1024 devices in a mesh: seq: 64 (over x, z_lo, core), head: 16 (over y, z_hi).
Axes of the slice: x: 4, y: 4, z: 32 (z_hi: 4, z_lo: 8; z = z_hi * 8 + z_lo), core: 2. Of those that a mesh axis runs over, the one named last changes fastest.
Arguments:
- queries: bfloat16 [16384, 64, 128], P('seq', 'head'), may hold values from -100 to 100
- key_states: bfloat16 [16384, 4, 128], P('seq'), may hold values from -6.7 to 6.7
- values: bfloat16 [16384, 4, 128], P('seq'), may hold values from -6 to 6
- grad_out: bfloat16 [16384, 64, 128], P('seq', 'head'), may hold values from -6 to 6
- picked_blocks: int32 [256, 4, 16], P('seq'), may hold values from -1 to 255, as said below
Outputs:
- grad_queries: float32 [16384, 64, 128], P('seq', 'head')
- grad_keys: float32 [16384, 4, 128], P(('seq', 'head'))
- grad_values: float32 [16384, 4, 128], P(('seq', 'head'))
The draws below stay inside these ranges and needn't reach their ends.
Inputs may be any that keep to these rules, and one draw needn't show every extreme that they name: picked_blocks[b, g, 0] = b. The query blocks come in runs of 256 / 64 (run s holds blocks s * 4 onward); for each run s and group g, the entries j >= 1 of the run's blocks that are not -1 name blocks of distinct runs, all lower than s, and there are exactly min(s, 60) of them.
All inputs are finite; a program needn't handle non-finite values.
Results may differ from the reference program's by a relative error of at most 0.02.
Values may be sent and summed in bfloat16 or wider, within the bound.
No kernel may reach another device: no remote copies, remote signals or barrier semaphores. Data moves between devices by JAX's collectives and lax.ppermute only.
A program may use at most 64 MiB of HBM per device.

```python
import jax
import jax.numpy as jnp
from jax import lax

G = 4
HPG = 16
DQK = 128
DV = 128
BLK = 64
KSEL = 16
TOK_DEV = 256
H = 64
TOKENS = 16384
N_HEAD = 16


def attention_pair(key):
    base_key = jax.random.fold_in(key, 11)
    key_first, key_second = jax.random.split(base_key, 2)
    key_values = jnp.clip(jax.random.normal(key_first, (TOKENS, G, DQK), jnp.float32), -6.0, 6.0)
    query_values = jnp.clip(jax.random.normal(key_second, (TOKENS, G * HPG, DQK), jnp.float32), -6.0, 6.0)
    return (query_values, key_values)


def draw_queries(key, part):
    return attention_pair(key)[0].astype(jnp.bfloat16)


def draw_key_states(key, part):
    return attention_pair(key)[1].astype(jnp.bfloat16)


def draw_picked_blocks(key, part):
    per_shard = TOK_DEV // BLK
    block_total = TOKENS // BLK
    shard_total = block_total // per_shard
    slot_total = per_shard * (KSEL - 1)
    live_total = min(slot_total, shard_total)
    base_key = jax.random.fold_in(key, 23)
    order_key, within_key = jax.random.split(base_key)
    seed_keys = jax.random.split(order_key, shard_total * G)
    orders = jax.vmap(lambda single: jax.random.permutation(single, shard_total))(seed_keys)
    orders = orders.astype(jnp.int32).reshape(shard_total, G, shard_total)
    shard_ids = jnp.arange(shard_total, dtype=jnp.int32)
    earlier = shard_ids[None, None, :] < shard_ids[:, None, None]
    scores = jnp.where(earlier, orders, -1 - shard_ids[None, None, :])
    best_score, where_from = lax.top_k(scores, live_total)
    within = jax.random.randint(within_key, (shard_total, G, live_total), 0, per_shard)
    chosen = jnp.where(best_score >= 0, where_from.astype(jnp.int32) * per_shard + within, -1).astype(jnp.int32)
    padding = jnp.full((shard_total, G, slot_total - live_total), -1, jnp.int32)
    chosen = jnp.concatenate([chosen, padding], axis=2)
    chosen = chosen.reshape(shard_total, G, KSEL - 1, per_shard).transpose(0, 3, 1, 2).reshape(block_total, G, KSEL - 1)
    self_block = jnp.broadcast_to(jnp.arange(block_total, dtype=jnp.int32)[:, None, None], (block_total, G, 1))
    return jnp.concatenate([self_block, chosen], axis=2)


def level_of(rng, shape, shards, low, high):
    gain, own = 1.0, jax.random.fold_in(rng, 6)
    for dim, shards_of in shards:
        steps = jnp.exp(jax.random.uniform(jax.random.fold_in(own, dim), (shards_of,), jnp.float32, low / len(shards), high / len(shards)))
        gain = gain * jnp.repeat(steps, shape[dim] // shards_of).reshape([-1 if axis == dim else 1 for axis in range(len(shape))])
    return gain


def gaussian(own_key, dims, deviation, limit, cuts=(), kind=jnp.bfloat16):
    array = jax.random.normal(own_key, dims, jnp.float32) * deviation
    if len(cuts) > 0:
        array = level_of(own_key, dims, cuts, -0.22, 0.18) * array
    return jnp.clip(array, min=-limit, max=limit).astype(kind)


def setup_inputs(seed: int = 0) -> dict:
    splits = jax.random.split(jax.random.key(seed), 6)
    queries = draw_queries(jax.random.fold_in(splits[5], 71), 0)
    key_states = draw_key_states(jax.random.fold_in(splits[5], 71), 0)
    values = gaussian(splits[2], (TOKENS, G, DV), 1.0, 6.0, ((0, 64),))
    grad_out = gaussian(splits[3], (TOKENS, H, DV), 1.0, 6.0, ((0, 64), (1, 16)))
    picked_blocks = draw_picked_blocks(jax.random.fold_in(splits[5], 71), 0)
    return dict(queries=queries, key_states=key_states, values=values, grad_out=grad_out, picked_blocks=picked_blocks)


NEG = -1.0e30


def reference(queries, key_states, values, grad_out, picked_blocks):
    factor = DQK ** -0.5
    block_total = TOKENS // BLK
    head_dev = (G * HPG) // N_HEAD
    spans = HPG // head_dev
    key_table = key_states.reshape(block_total, BLK, G, DQK).transpose(2, 0, 1, 3)
    value_table = values.reshape(block_total, BLK, G, DV).transpose(2, 0, 1, 3)
    query_blocks = queries.reshape(block_total, BLK, G, HPG, DQK)
    grad_blocks = grad_out.reshape(block_total, BLK, G, HPG, DV)
    group_index = jnp.arange(G, dtype=jnp.int32)[:, None]
    offsets = jnp.arange(BLK, dtype=jnp.int32)
    causal = offsets[None, :] <= offsets[:, None]
    leading = jnp.arange(KSEL, dtype=jnp.int32) == 0

    def accumulate(carry, inputs):
        key_accum, value_accum = carry
        query_block, grad_block, pick_row = inputs
        live_slots = pick_row >= 0
        safe_pick = jnp.maximum(pick_row, 0).astype(jnp.int32)
        key_sets = key_table[group_index, safe_pick]
        value_sets = value_table[group_index, safe_pick]
        query_wide = query_block.astype(jnp.float32)
        grad_wide = grad_block.astype(jnp.float32)
        key_wide = key_sets.astype(jnp.float32)
        value_wide = value_sets.astype(jnp.float32)
        scores = jnp.einsum("tghd,gjkd->ghtjk", query_wide, key_wide) * factor
        visible = live_slots[:, None, None, :, None] & (jnp.logical_not(leading)[None, None, None, :, None] | causal[None, None, :, None, :])
        scores = jnp.where(visible, scores, NEG)
        maxima = jnp.max(scores, axis=(3, 4), keepdims=True)
        weights = jnp.where(visible, jnp.exp(scores - maxima), 0.0)
        attend = weights / jnp.sum(weights, axis=(3, 4), keepdims=True)
        attend_low = attend.astype(jnp.bfloat16)
        grad_prob = jnp.einsum("tghe,gjke->ghtjk", grad_wide, value_wide)
        row_dot = jnp.sum(attend * grad_prob, axis=(3, 4), keepdims=True)
        dscore = (attend * (grad_prob - row_dot)).astype(jnp.bfloat16)
        dscore_wide = dscore.astype(jnp.float32)
        grad_query = jnp.einsum("ghtjk,gjkd->tghd", dscore_wide, key_wide) * factor
        dscore_runs = dscore_wide.reshape(G, spans, head_dev, BLK, KSEL, BLK)
        attend_runs = attend_low.astype(jnp.float32).reshape(G, spans, head_dev, BLK, KSEL, BLK)
        query_runs = query_wide.reshape(BLK, G, spans, head_dev, DQK)
        grad_runs = grad_wide.reshape(BLK, G, spans, head_dev, DV)
        key_parts = jnp.einsum("gchtjk,tgchd->gcjkd", dscore_runs, query_runs) * factor
        value_parts = jnp.einsum("gchtjk,tgche->gcjke", attend_runs, grad_runs)
        key_rounded = lax.optimization_barrier(key_parts.astype(jnp.bfloat16)).astype(jnp.float32)
        value_rounded = lax.optimization_barrier(value_parts.astype(jnp.bfloat16)).astype(jnp.float32)
        key_contrib = jnp.where(leading[None, :, None, None], key_parts.sum(axis=1), key_rounded.sum(axis=1))
        value_contrib = jnp.where(leading[None, :, None, None], value_parts.sum(axis=1), value_rounded.sum(axis=1))
        target = jnp.where(live_slots, pick_row, block_total).astype(jnp.int32)
        key_accum = key_accum.at[group_index, target].add(key_contrib, mode="drop")
        value_accum = value_accum.at[group_index, target].add(value_contrib, mode="drop")
        return (key_accum, value_accum), grad_query

    start = (jnp.zeros((G, block_total, BLK, DQK), jnp.float32), jnp.zeros((G, block_total, BLK, DV), jnp.float32))
    finals, grad_query_blocks = lax.scan(accumulate, start, (query_blocks, grad_blocks, picked_blocks))
    key_accum, value_accum = finals
    grad_queries = grad_query_blocks.reshape(TOKENS, G * HPG, DQK)
    grad_keys = key_accum.transpose(1, 2, 0, 3).reshape(TOKENS, G, DQK)
    grad_values = value_accum.transpose(1, 2, 0, 3).reshape(TOKENS, G, DV)
    return (grad_queries, grad_keys, grad_values)
```

```python
import functools

import jax
import jax.numpy as jnp
from jax import lax
from jax.experimental import pallas as pl
from jax.experimental.pallas import tpu as pltpu
from jax.sharding import Mesh
from jax.sharding import PartitionSpec as P

HPG = 16
BLK = 64
KSEL = 16
NEG = -1e30

NX, ZL, NC, NY, ZH = 4, 8, 2, 4, 4
NZ = ZL * ZH
SEQ = ("x", "zl", "c")
HEAD = ("y", "zh")
XC = ("x", "c")
AXES = SEQ + HEAD

F32 = jnp.float32
BF16 = jnp.bfloat16


def ring_pairs(step):
    def number(x, z, c, y):
        return (((x * ZL + z % ZL) * NC + c) * NY + y) * ZH + z // ZL

    return [
        (number(x, z, c, y), number(x, (z + step) % NZ, c, y))
        for x in range(NX)
        for z in range(NZ)
        for c in range(NC)
        for y in range(NY)
    ]


def shift_z(array, step):
    return lax.ppermute(array, AXES, ring_pairs(step))


def attend_body(slot_ref, q_ref, g_ref, own_ref, bias_ref, got_ref, dq_ref, down_ref, back_ref, k_ref, v_ref):
    b = pl.program_id(0)
    rows = q_ref.shape[0]
    width = q_ref.shape[1]
    heads = rows // BLK
    factor = width ** (-0.5)

    @pl.when(b == 0)
    def _():
        back_ref[...] = jnp.zeros_like(back_ref)

    k_ref[0:BLK, :] = own_ref[0, :, :width]
    v_ref[0:BLK, :] = own_ref[0, :, width:]
    for j in range(1, KSEL):
        slot = jnp.maximum(slot_ref[b, j], 0)
        k_ref[j * BLK : (j + 1) * BLK, :] = got_ref[slot, :, :width]
        v_ref[j * BLK : (j + 1) * BLK, :] = got_ref[slot, :, width:]
    q = q_ref[...]
    g = g_ref[...]
    k = k_ref[...]
    v = v_ref[...]
    nt = (((1,), (1,)), ((), ()))
    scores = lax.dot_general(k, q, nt, preferred_element_type=F32) * factor
    key_row = lax.broadcasted_iota(jnp.int32, (BLK, rows), 0)
    token = lax.broadcasted_iota(jnp.int32, (BLK, rows), 1) // heads
    own = jnp.where(key_row <= token, scores[:BLK], NEG)
    far = scores[BLK:].reshape(KSEL - 1, BLK, rows) + bias_ref[0, 1:][:, None, :]
    scores = jnp.concatenate([own, far.reshape((KSEL - 1) * BLK, rows)], axis=0)
    weights = jnp.exp(scores - jnp.max(scores, axis=0, keepdims=True))
    attend = weights * (1.0 / jnp.sum(weights, axis=0, keepdims=True))
    grad_prob = lax.dot_general(v, g, nt, preferred_element_type=F32)
    row_dot = jnp.sum(attend * grad_prob, axis=0, keepdims=True)
    dscore = (attend * (grad_prob - row_dot)).astype(BF16)
    tn = (((0,), (0,)), ((), ()))
    nn = (((1,), (0,)), ((), ()))
    dq = lax.dot_general(k, dscore, tn, preferred_element_type=F32) * factor
    dq_ref[...] = dq.T
    dk = lax.dot_general(dscore, q, nn, preferred_element_type=F32) * factor
    dv = lax.dot_general(attend.astype(BF16), g, nn, preferred_element_type=F32)
    down_ref[0, :, :width] = dk[:BLK]
    down_ref[0, :, width:] = dv[:BLK]
    for j in range(1, KSEL):
        slot = slot_ref[b, j]

        @pl.when(slot >= 0)
        def _():
            back_ref[slot, :, :width] = dk[j * BLK : (j + 1) * BLK].astype(BF16)
            back_ref[slot, :, width:] = dv[j * BLK : (j + 1) * BLK].astype(BF16)


def attend_grads(slots, q_rows, g_rows, own, bias, got):
    blocks = slots.shape[0]
    total, width = q_rows.shape
    rows = total // blocks
    row_spec = pl.BlockSpec((rows, width), lambda b, s: (b, 0))
    own_spec = pl.BlockSpec((1, BLK, 2 * width), lambda b, s: (b, 0, 0))
    whole = pl.BlockSpec(got.shape, lambda b, s: (0, 0, 0))
    return pl.pallas_call(
        attend_body,
        grid_spec=pltpu.PrefetchScalarGridSpec(
            num_scalar_prefetch=1,
            grid=(blocks,),
            in_specs=[row_spec, row_spec, own_spec, pl.BlockSpec((1, KSEL, rows), lambda b, s: (b, 0, 0)), whole],
            out_specs=[row_spec, own_spec, whole],
            scratch_shapes=[pltpu.VMEM((KSEL * BLK, width), BF16), pltpu.VMEM((KSEL * BLK, width), BF16)],
        ),
        out_shape=[
            jax.ShapeDtypeStruct((total, width), F32),
            jax.ShapeDtypeStruct((blocks, BLK, 2 * width), F32),
            jax.ShapeDtypeStruct(got.shape, BF16),
        ],
        compiler_params=pltpu.CompilerParams(dimension_semantics=("arbitrary",), vmem_limit_bytes=48 * 2**20),
        name="attend_grads",
    )(slots, q_rows, g_rows, own, bias, got)


def pick_body(want_ref, home_ref, *refs):
    out_ref = refs[-1]
    for k, near_ref in enumerate(refs[:-1]):
        zl = lax.rem(home_ref[0] + k, ZL)
        for peer in range(NX * NC):
            slot = jnp.maximum(want_ref[peer, zl], 0)
            out_ref[peer, zl] = near_ref[slot]


def pick_blocks(want, home, near):
    blocks, rows, width = near[0].shape
    shape = (NX * NC, ZL, rows, width)
    spec = pl.BlockSpec((blocks, rows, width), lambda i, w, h: (0, 0, 0))
    return pl.pallas_call(
        pick_body,
        grid_spec=pltpu.PrefetchScalarGridSpec(
            num_scalar_prefetch=2,
            grid=(1,),
            in_specs=[spec] * ZL,
            out_specs=pl.BlockSpec(shape, lambda i, w, h: (0, 0, 0, 0)),
        ),
        out_shape=jax.ShapeDtypeStruct(shape, near[0].dtype),
        compiler_params=pltpu.CompilerParams(vmem_limit_bytes=32 * 2**20),
        name="pick_blocks",
    )(want, home, *near)


def gather_body(want_ref, home_ref, in_ref, out_ref, sum_ref):
    zl = lax.rem(home_ref[0] + pl.program_id(0), ZL)
    sum_ref[...] = jnp.zeros_like(sum_ref)
    for peer in range(NX * NC):
        slot = want_ref[peer, zl]

        @pl.when(slot >= 0)
        def _():
            sum_ref[slot] += in_ref[peer, 0].astype(F32)

    out_ref[0] = sum_ref[...].astype(out_ref.dtype)


def sum_parts(want, home, parts, blocks):
    peers, runs, rows, width = parts.shape
    return pl.pallas_call(
        gather_body,
        grid_spec=pltpu.PrefetchScalarGridSpec(
            num_scalar_prefetch=2,
            grid=(runs,),
            in_specs=[
                pl.BlockSpec((peers, 1, rows, width), lambda k, w, h: (0, lax.rem(h[0] + k, ZL), 0, 0)),
            ],
            out_specs=pl.BlockSpec((1, blocks, rows, width), lambda k, w, h: (k, 0, 0, 0)),
            scratch_shapes=[pltpu.VMEM((blocks, rows, width), F32)],
        ),
        out_shape=jax.ShapeDtypeStruct((runs, blocks, rows, width), BF16),
        compiler_params=pltpu.CompilerParams(dimension_semantics=("arbitrary",)),
        name="sum_parts",
    )(want, home, parts)


def on_device(queries, key_states, values, grad_out, picked_blocks):
    tokens, heads, width = queries.shape
    blocks = tokens // BLK
    group = lax.axis_index("y")
    home = lax.axis_index("zl").astype(jnp.int32)[None]
    own_keys = lax.dynamic_index_in_dim(key_states, group, 1, keepdims=False)
    own_values = lax.dynamic_index_in_dim(values, group, 1, keepdims=False)
    own = jnp.concatenate([own_keys, own_values], axis=1).reshape(blocks, BLK, 2 * width)
    picks = lax.dynamic_index_in_dim(picked_blocks, group, 1, keepdims=False)

    near = [None] * ZL
    near[0] = own
    ahead = behind = own
    for step in range(1, ZL // 2 + 1):
        ahead = shift_z(ahead, 1)
        near[ZL - step] = ahead
        if step < ZL // 2:
            behind = shift_z(behind, -1)
            near[step] = behind

    live = picks >= 0
    run = jnp.where(live, picks // blocks, -1)
    run_ids = jnp.arange(NX * ZL * NC, dtype=jnp.int32)
    match = run[:, 1:, None] == run_ids
    wanted = jnp.max(jnp.where(match, (picks % blocks)[:, 1:, None], -1), axis=(0, 1))
    wanted = wanted.reshape(NX, ZL, NC).transpose(0, 2, 1).reshape(NX * NC, ZL)
    asked = lax.all_to_all(wanted, XC, split_axis=0, concat_axis=0, tiled=True)

    sent = pick_blocks(asked, home, near)
    got = lax.all_to_all(sent, XC, split_axis=0, concat_axis=0, tiled=True)
    got = got.reshape(NX * NC * ZL, BLK, 2 * width)
    run_x, run_z, run_c = run // (ZL * NC), run // NC % ZL, run % NC
    slots = jnp.where(live, (run_x * NC + run_c) * ZL + run_z, -1)
    bias = jnp.where(live, 0.0, NEG).astype(F32)
    bias = jnp.broadcast_to(bias[:, :, None], (blocks, KSEL, BLK * heads))
    dq, own_grads, back = attend_grads(
        slots, queries.reshape(tokens * heads, width), grad_out.reshape(tokens * heads, width), own, bias, got
    )
    grad_queries = dq.reshape(tokens, heads, width)

    parts = lax.all_to_all(back.reshape(NX * NC, ZL, BLK, 2 * width), XC, split_axis=0, concat_axis=0, tiled=True)
    sums = sum_parts(asked, home, parts, blocks)

    ahead = sums[ZL // 2]
    behind = None
    for step in range(ZL // 2, 0, -1):
        ahead = shift_z(ahead, 1)
        if step > 1:
            ahead = (ahead.astype(F32) + sums[step - 1].astype(F32)).astype(BF16)
        if step < ZL // 2:
            behind = sums[ZL - step] if behind is None else (behind.astype(F32) + sums[ZL - step].astype(F32)).astype(BF16)
            behind = shift_z(behind, -1)
    total = own_grads + sums[0].astype(F32) + ahead.astype(F32) + behind.astype(F32)

    pieces = total.astype(BF16).reshape(NY * ZH, tokens // (NY * ZH), 2 * width)
    pieces = lax.all_to_all(pieces, HEAD, split_axis=0, concat_axis=0, tiled=True)
    summed = pieces.astype(F32).reshape(NY, ZH, tokens // (NY * ZH), 2 * width).sum(axis=1)
    summed = summed.transpose(1, 0, 2)
    return (grad_queries, summed[:, :, :width], summed[:, :, width:])


def solution(mesh):
    torus = Mesh(mesh.devices.reshape(NX, ZL, NC, NY, ZH), AXES)
    by_head = P(SEQ, HEAD, None)
    by_run = P(SEQ, None, None)
    by_all = P(AXES, None, None)
    return jax.shard_map(
        on_device,
        mesh=torus,
        in_specs=(by_head, by_run, by_run, by_head, by_run),
        out_specs=(by_head, by_all, by_all),
        check_vma=False,
    )
```

```python
import functools

import jax
import jax.numpy as jnp
from jax import lax
from jax.experimental import pallas as pl
from jax.experimental.pallas import tpu as pltpu
from jax.sharding import Mesh
from jax.sharding import PartitionSpec as P

BLK = 64
KSEL = 16
NEG = -1e30

NX, ZL, NC, NY, ZH = 4, 8, 2, 4, 4
NZ = ZL * ZH
SEQ = ("x", "zl", "c")
HEAD = ("y", "zh")
XC = ("x", "c")
AXES = SEQ + HEAD
NEAR = ZL // 2
PARTS = 1
PER = NEAR // PARTS

F32 = jnp.float32
BF16 = jnp.bfloat16


def number(x, z, c, y):
    return (((x * ZL + z % ZL) * NC + c) * NY + y) * ZH + z % NZ // ZL


def send(array, move):
    pairs = []
    for x in range(NX):
        for z in range(NZ):
            for c in range(NC):
                for y in range(NY):
                    to = move(c)
                    if to is not None:
                        pairs.append((number(x, z, c, y), number(x, z + to[0], to[1], y)))
    return lax.ppermute(array, AXES, pairs)


def swap_cores(c):
    return (0, 1 - c)


def spread(c):
    return (1 if c == 0 else -1, c)


def spread_last(c):
    return (1, 0) if c == 0 else None


def collect(c):
    return (-1 if c == 0 else 1, c)


def collect_same(c):
    return (-1, 0) if c == 0 else None


def collect_cross(c):
    return (-1, 1) if c == 0 else (0, 0)


def attend_body(slot_ref, q_ref, g_ref, own_ref, bias_ref, *refs):
    got_refs = refs[:PARTS]
    dq_ref, down_ref = refs[PARTS : PARTS + 2]
    back_refs = refs[PARTS + 2 : 2 * PARTS + 2]
    k_ref, v_ref = refs[2 * PARTS + 2 :]
    held = got_refs[0].shape[0]
    b = pl.program_id(0)
    rows = q_ref.shape[0]
    width = q_ref.shape[1]
    heads = rows // BLK
    factor = width ** (-0.5)

    @pl.when(b == 0)
    def _():
        for back_ref in back_refs:
            back_ref[...] = jnp.zeros_like(back_ref)

    k_ref[0:BLK, :] = own_ref[0, :, :width]
    v_ref[0:BLK, :] = own_ref[0, :, width:]
    for j in range(1, KSEL):
        slot = jnp.maximum(slot_ref[b, j], 0)
        for part, got_ref in enumerate(got_refs):

            @pl.when(slot // held == part)
            def _():
                k_ref[j * BLK : (j + 1) * BLK, :] = got_ref[slot - part * held, :, :width]
                v_ref[j * BLK : (j + 1) * BLK, :] = got_ref[slot - part * held, :, width:]

    q = q_ref[...]
    g = g_ref[...]
    k = k_ref[...]
    v = v_ref[...]
    nt = (((1,), (1,)), ((), ()))
    scores = lax.dot_general(k, q, nt, preferred_element_type=F32) * factor
    key_row = lax.broadcasted_iota(jnp.int32, (BLK, rows), 0)
    token = lax.broadcasted_iota(jnp.int32, (BLK, rows), 1) // heads
    own = jnp.where(key_row <= token, scores[:BLK], NEG)
    far = scores[BLK:].reshape(KSEL - 1, BLK, rows) + bias_ref[0, 1:][:, None, :]
    scores = jnp.concatenate([own, far.reshape((KSEL - 1) * BLK, rows)], axis=0)
    weights = jnp.exp(scores - jnp.max(scores, axis=0, keepdims=True))
    attend = weights * (1.0 / jnp.sum(weights, axis=0, keepdims=True))
    grad_prob = lax.dot_general(v, g, nt, preferred_element_type=F32)
    row_dot = jnp.sum(attend * grad_prob, axis=0, keepdims=True)
    dscore = (attend * (grad_prob - row_dot)).astype(BF16)
    tn = (((0,), (0,)), ((), ()))
    nn = (((1,), (0,)), ((), ()))
    dq = lax.dot_general(k, dscore, tn, preferred_element_type=F32) * factor
    dq_ref[...] = dq.T
    dk = lax.dot_general(dscore, q, nn, preferred_element_type=F32) * factor
    dv = lax.dot_general(attend.astype(BF16), g, nn, preferred_element_type=F32)
    down_ref[0, :, :width] = dk[:BLK]
    down_ref[0, :, width:] = dv[:BLK]
    for j in range(1, KSEL):
        slot = slot_ref[b, j]

        for part, back_ref in enumerate(back_refs):

            @pl.when((slot >= part * held) & (slot < (part + 1) * held))
            def _():
                back_ref[slot - part * held, :, :width] = dk[j * BLK : (j + 1) * BLK].astype(BF16)
                back_ref[slot - part * held, :, width:] = dv[j * BLK : (j + 1) * BLK].astype(BF16)


def attend_grads(slots, q_rows, g_rows, own, bias, got):
    blocks = slots.shape[0]
    total, width = q_rows.shape
    rows = total // blocks
    row_spec = pl.BlockSpec((rows, width), lambda b, s: (b, 0))
    own_spec = pl.BlockSpec((1, BLK, 2 * width), lambda b, s: (b, 0, 0))
    whole = pl.BlockSpec(got[0].shape, lambda b, s: (0, 0, 0))
    return pl.pallas_call(
        attend_body,
        grid_spec=pltpu.PrefetchScalarGridSpec(
            num_scalar_prefetch=1,
            grid=(blocks,),
            in_specs=[row_spec, row_spec, own_spec, pl.BlockSpec((1, KSEL, rows), lambda b, s: (b, 0, 0))]
            + [whole] * PARTS,
            out_specs=[row_spec, own_spec] + [whole] * PARTS,
            scratch_shapes=[pltpu.VMEM((KSEL * BLK, width), BF16), pltpu.VMEM((KSEL * BLK, width), BF16)],
        ),
        out_shape=[
            jax.ShapeDtypeStruct((total, width), F32),
            jax.ShapeDtypeStruct((blocks, BLK, 2 * width), F32),
        ]
        + [jax.ShapeDtypeStruct(got[0].shape, BF16)] * PARTS,
        compiler_params=pltpu.CompilerParams(dimension_semantics=("arbitrary",), vmem_limit_bytes=48 * 2**20),
        name="attend_grads",
    )(slots, q_rows, g_rows, own, bias, *got)


def pick_body(part, want_ref, core_ref, *refs):
    out_ref = refs[-1]
    for core in range(NC):

        @pl.when(core_ref[0] == core)
        def _():
            for step in range(PER):
                near_ref = refs[step + 1 - core]
                for which in range(NC):
                    for peer in range(NX * NC):
                        slot = want_ref[peer, (part * PER + step) * NC + which]
                        out_ref[peer, step * NC + which] = near_ref[which, jnp.maximum(slot, 0)]


def pick_blocks(part, want, core, near):
    cores, blocks, rows, width = near[0].shape
    shape = (NX * NC, PER * NC, rows, width)
    spec = pl.BlockSpec(near[0].shape, lambda i, w, h: (0, 0, 0, 0))
    return pl.pallas_call(
        functools.partial(pick_body, part),
        grid_spec=pltpu.PrefetchScalarGridSpec(
            num_scalar_prefetch=2,
            grid=(1,),
            in_specs=[spec] * (PER + 1),
            out_specs=pl.BlockSpec(shape, lambda i, w, h: (0, 0, 0, 0)),
        ),
        out_shape=jax.ShapeDtypeStruct(shape, near[0].dtype),
        compiler_params=pltpu.CompilerParams(vmem_limit_bytes=32 * 2**20),
        name="pick_blocks",
    )(want, core, *near[part * PER : (part + 1) * PER + 1])


def sum_body(part, want_ref, in_ref, *refs):
    sum_ref = refs[-1]
    for step in range(PER):
        for which in range(NC):
            sum_ref[...] = jnp.zeros_like(sum_ref)
            for peer in range(NX * NC):
                slot = jnp.maximum(want_ref[peer, (part * PER + step) * NC + which], 0)
                sum_ref[slot] += in_ref[peer, step * NC + which].astype(F32)
            refs[step][which] = sum_ref[...].astype(BF16)


def sum_parts(part, want, parts, blocks):
    peers, runs, rows, width = parts.shape
    shape = (NC, blocks, rows, width)
    return pl.pallas_call(
        functools.partial(sum_body, part),
        grid_spec=pltpu.PrefetchScalarGridSpec(
            num_scalar_prefetch=1,
            grid=(1,),
            in_specs=[pl.BlockSpec(parts.shape, lambda k, w: (0, 0, 0, 0))],
            out_specs=[pl.BlockSpec(shape, lambda k, w: (0, 0, 0, 0))] * PER,
            scratch_shapes=[pltpu.VMEM((blocks, rows, width), F32)],
        ),
        out_shape=[jax.ShapeDtypeStruct(shape, BF16)] * PER,
        compiler_params=pltpu.CompilerParams(vmem_limit_bytes=32 * 2**20),
        name="sum_parts",
    )(want, parts)


def plus(a, b):
    return (a.astype(F32) + b.astype(F32)).astype(BF16)


def on_device(queries, key_states, values, grad_out, picked_blocks):
    tokens, heads, width = queries.shape
    blocks = tokens // BLK
    group = lax.axis_index("y")
    core = lax.axis_index("c").astype(jnp.int32)
    home = lax.axis_index("zl").astype(jnp.int32)
    own_keys = lax.dynamic_index_in_dim(key_states, group, 1, keepdims=False)
    own_values = lax.dynamic_index_in_dim(values, group, 1, keepdims=False)
    own = jnp.concatenate([own_keys, own_values], axis=1).reshape(1, blocks, BLK, 2 * width)
    picks = lax.dynamic_index_in_dim(picked_blocks, group, 1, keepdims=False)

    live = picks >= 0
    run = picks // blocks
    ahead = lax.rem(run // NC % ZL - home + ZL, ZL)
    holder = (ahead < NEAR).astype(jnp.int32)
    step = jnp.where(holder == 1, ahead, ZL - 1 - ahead)
    which = jnp.where(run % NC == holder, 0, 1)
    peer = run // (ZL * NC) * NC + holder
    place = jnp.where(live, peer * ZL + step * NC + which, -1)
    match = place[:, 1:, None] == jnp.arange(NX * ZL * NC, dtype=jnp.int32)
    wanted = jnp.max(jnp.where(match, (picks % blocks)[:, 1:, None], -1), axis=(0, 1))
    wanted = wanted.reshape(NX * NC, ZL)
    asked = lax.all_to_all(wanted, XC, split_axis=0, concat_axis=0, tiled=True)

    near = [jnp.concatenate([own, send(own, swap_cores)], axis=0)]
    for turn in range(NEAR):
        near.append(send(near[-1], spread if turn < NEAR - 1 else spread_last))

    got = []
    for part in range(PARTS):
        sent = pick_blocks(part, asked, core[None], near)
        arrived = lax.all_to_all(sent, XC, split_axis=0, concat_axis=0, tiled=True)
        got.append(arrived.reshape(NX * NC * PER * NC, BLK, 2 * width))
    slots = (step // PER * (NX * NC) + peer) * (PER * NC) + step % PER * NC + which
    slots = jnp.where(live, slots, -1)
    bias = jnp.where(live, 0.0, NEG).astype(F32)
    bias = jnp.broadcast_to(bias[:, :, None], (blocks, KSEL, BLK * heads))
    dq, own_grads, *back = attend_grads(
        slots, queries.reshape(tokens * heads, width), grad_out.reshape(tokens * heads, width), own[0], bias, got
    )
    grad_queries = dq.reshape(tokens, heads, width)

    sums = [None] * NEAR
    for part in reversed(range(PARTS)):
        parts = back[part].reshape(NX * NC, PER * NC, BLK, 2 * width)
        parts = lax.all_to_all(parts, XC, split_axis=0, concat_axis=0, tiled=True)
        sums[part * PER : (part + 1) * PER] = sum_parts(part, asked, parts, blocks)
    chain = sums[NEAR - 1]
    for turn in range(NEAR - 2, -1, -1):
        chain = plus(send(chain, collect), sums[turn])
    same = send(chain[0], collect_same)
    cross = send(chain[1], collect_cross)
    same = jnp.where(core == 0, same, chain[0])
    total = own_grads + same.astype(F32) + cross.astype(F32)

    pieces = total.astype(BF16).reshape(NY * ZH, tokens // (NY * ZH), 2 * width)
    pieces = lax.all_to_all(pieces, HEAD, split_axis=0, concat_axis=0, tiled=True)
    summed = pieces.astype(F32).reshape(NY, ZH, tokens // (NY * ZH), 2 * width).sum(axis=1)
    summed = summed.transpose(1, 0, 2)
    return (grad_queries, summed[:, :, :width], summed[:, :, width:])


def solution(mesh):
    torus = Mesh(mesh.devices.reshape(NX, ZL, NC, NY, ZH), AXES)
    by_head = P(SEQ, HEAD, None)
    by_run = P(SEQ, None, None)
    by_all = P(AXES, None, None)
    return jax.shard_map(
        on_device,
        mesh=torus,
        in_specs=(by_head, by_run, by_run, by_head, by_run),
        out_specs=(by_head, by_all, by_all),
        check_vma=False,
    )
```

```python
import functools

import jax
import jax.numpy as jnp
from jax import lax
from jax.experimental import pallas as pl
from jax.experimental.pallas import tpu as pltpu
from jax.sharding import Mesh
from jax.sharding import PartitionSpec as P

BLK = 64
KSEL = 16
NEG = -1e30

NX, ZL, NC, NY, ZH = 4, 8, 2, 4, 4
NZ = ZL * ZH
SEQ = ("x", "zl", "c")
HEAD = ("y", "zh")
XC = ("x", "c")
AXES = SEQ + HEAD
NEAR = ZL // 2
PARTS = 2
PER = NEAR // PARTS

F32 = jnp.float32
BF16 = jnp.bfloat16


def number(x, z, c, y):
    return (((x * ZL + z % ZL) * NC + c) * NY + y) * ZH + z % NZ // ZL


def send(array, move):
    pairs = []
    for x in range(NX):
        for z in range(NZ):
            for c in range(NC):
                for y in range(NY):
                    to = move(c)
                    if to is not None:
                        pairs.append((number(x, z, c, y), number(x, z + to[0], to[1], y)))
    return lax.ppermute(array, AXES, pairs)


def swap_cores(c):
    return (0, 1 - c)


def spread(c):
    return (1 if c == 0 else -1, c)


def spread_last(c):
    return (1, 0) if c == 0 else None


def collect(c):
    return (-1 if c == 0 else 1, c)


def collect_same(c):
    return (-1, 0) if c == 0 else None


def collect_cross(c):
    return (-1, 1) if c == 0 else (0, 0)


def attend_body(slot_ref, q_ref, g_ref, own_ref, bias_ref, *refs):
    got_refs = refs[:PARTS]
    dq_ref, down_ref = refs[PARTS : PARTS + 2]
    back_refs = refs[PARTS + 2 : 2 * PARTS + 2]
    k_ref, v_ref = refs[2 * PARTS + 2 :]
    held = got_refs[0].shape[0]
    b = pl.program_id(0)
    rows = q_ref.shape[0]
    width = q_ref.shape[1]
    heads = rows // BLK
    factor = width ** (-0.5)

    @pl.when(b == 0)
    def _():
        for back_ref in back_refs:
            back_ref[...] = jnp.zeros_like(back_ref)

    k_ref[0:BLK, :] = own_ref[0, :, :width]
    v_ref[0:BLK, :] = own_ref[0, :, width:]
    for j in range(1, KSEL):
        slot = jnp.maximum(slot_ref[b, j], 0)
        for part, got_ref in enumerate(got_refs):

            @pl.when(slot // held == part)
            def _():
                k_ref[j * BLK : (j + 1) * BLK, :] = got_ref[slot - part * held, :, :width]
                v_ref[j * BLK : (j + 1) * BLK, :] = got_ref[slot - part * held, :, width:]

    q = q_ref[...]
    g = g_ref[...]
    k = k_ref[...]
    v = v_ref[...]
    nt = (((1,), (1,)), ((), ()))
    scores = lax.dot_general(k, q, nt, preferred_element_type=F32) * factor
    key_row = lax.broadcasted_iota(jnp.int32, (BLK, rows), 0)
    token = lax.broadcasted_iota(jnp.int32, (BLK, rows), 1) // heads
    own = jnp.where(key_row <= token, scores[:BLK], NEG)
    far = scores[BLK:].reshape(KSEL - 1, BLK, rows) + bias_ref[0, 1:][:, None, :]
    scores = jnp.concatenate([own, far.reshape((KSEL - 1) * BLK, rows)], axis=0)
    weights = jnp.exp(scores - jnp.max(scores, axis=0, keepdims=True))
    attend = weights * (1.0 / jnp.sum(weights, axis=0, keepdims=True))
    grad_prob = lax.dot_general(v, g, nt, preferred_element_type=F32)
    row_dot = jnp.sum(attend * grad_prob, axis=0, keepdims=True)
    dscore = (attend * (grad_prob - row_dot)).astype(BF16)
    tn = (((0,), (0,)), ((), ()))
    nn = (((1,), (0,)), ((), ()))
    dq = lax.dot_general(k, dscore, tn, preferred_element_type=F32) * factor
    dq_ref[...] = dq.T
    dk = lax.dot_general(dscore, q, nn, preferred_element_type=F32) * factor
    dv = lax.dot_general(attend.astype(BF16), g, nn, preferred_element_type=F32)
    down_ref[0, :, :width] = dk[:BLK]
    down_ref[0, :, width:] = dv[:BLK]
    for j in range(1, KSEL):
        slot = slot_ref[b, j]

        for part, back_ref in enumerate(back_refs):

            @pl.when((slot >= part * held) & (slot < (part + 1) * held))
            def _():
                back_ref[slot - part * held, :, :width] = dk[j * BLK : (j + 1) * BLK].astype(BF16)
                back_ref[slot - part * held, :, width:] = dv[j * BLK : (j + 1) * BLK].astype(BF16)


def attend_grads(slots, q_rows, g_rows, own, bias, got):
    blocks = slots.shape[0]
    total, width = q_rows.shape
    rows = total // blocks
    row_spec = pl.BlockSpec((rows, width), lambda b, s: (b, 0))
    own_spec = pl.BlockSpec((1, BLK, 2 * width), lambda b, s: (b, 0, 0))
    whole = pl.BlockSpec(got[0].shape, lambda b, s: (0, 0, 0))
    return pl.pallas_call(
        attend_body,
        grid_spec=pltpu.PrefetchScalarGridSpec(
            num_scalar_prefetch=1,
            grid=(blocks,),
            in_specs=[row_spec, row_spec, own_spec, pl.BlockSpec((1, KSEL, rows), lambda b, s: (b, 0, 0))]
            + [whole] * PARTS,
            out_specs=[row_spec, own_spec] + [whole] * PARTS,
            scratch_shapes=[pltpu.VMEM((KSEL * BLK, width), BF16), pltpu.VMEM((KSEL * BLK, width), BF16)],
        ),
        out_shape=[
            jax.ShapeDtypeStruct((total, width), F32),
            jax.ShapeDtypeStruct((blocks, BLK, 2 * width), F32),
        ]
        + [jax.ShapeDtypeStruct(got[0].shape, BF16)] * PARTS,
        compiler_params=pltpu.CompilerParams(dimension_semantics=("arbitrary",), vmem_limit_bytes=48 * 2**20),
        name="attend_grads",
    )(slots, q_rows, g_rows, own, bias, *got)


def pick_body(part, want_ref, core_ref, *refs):
    out_ref = refs[-1]
    for core in range(NC):

        @pl.when(core_ref[0] == core)
        def _():
            for step in range(PER):
                near_ref = refs[step + 1 - core]
                for which in range(NC):
                    for peer in range(NX * NC):
                        slot = want_ref[peer, (part * PER + step) * NC + which]
                        out_ref[peer, step * NC + which] = near_ref[which, jnp.maximum(slot, 0)]


def pick_blocks(part, want, core, near):
    cores, blocks, rows, width = near[0].shape
    shape = (NX * NC, PER * NC, rows, width)
    spec = pl.BlockSpec(near[0].shape, lambda i, w, h: (0, 0, 0, 0))
    return pl.pallas_call(
        functools.partial(pick_body, part),
        grid_spec=pltpu.PrefetchScalarGridSpec(
            num_scalar_prefetch=2,
            grid=(1,),
            in_specs=[spec] * (PER + 1),
            out_specs=pl.BlockSpec(shape, lambda i, w, h: (0, 0, 0, 0)),
        ),
        out_shape=jax.ShapeDtypeStruct(shape, near[0].dtype),
        compiler_params=pltpu.CompilerParams(vmem_limit_bytes=32 * 2**20),
        name="pick_blocks",
    )(want, core, *near[part * PER : (part + 1) * PER + 1])


def sum_body(part, want_ref, in_ref, *refs):
    sum_ref = refs[-1]
    for step in range(PER):
        for which in range(NC):
            sum_ref[...] = jnp.zeros_like(sum_ref)
            for peer in range(NX * NC):
                slot = jnp.maximum(want_ref[peer, (part * PER + step) * NC + which], 0)
                sum_ref[slot] += in_ref[peer, step * NC + which].astype(F32)
            refs[step][which] = sum_ref[...].astype(BF16)


def sum_parts(part, want, parts, blocks):
    peers, runs, rows, width = parts.shape
    shape = (NC, blocks, rows, width)
    return pl.pallas_call(
        functools.partial(sum_body, part),
        grid_spec=pltpu.PrefetchScalarGridSpec(
            num_scalar_prefetch=1,
            grid=(1,),
            in_specs=[pl.BlockSpec(parts.shape, lambda k, w: (0, 0, 0, 0))],
            out_specs=[pl.BlockSpec(shape, lambda k, w: (0, 0, 0, 0))] * PER,
            scratch_shapes=[pltpu.VMEM((blocks, rows, width), F32)],
        ),
        out_shape=[jax.ShapeDtypeStruct(shape, BF16)] * PER,
        compiler_params=pltpu.CompilerParams(vmem_limit_bytes=32 * 2**20),
        name="sum_parts",
    )(want, parts)


def plus(a, b):
    return (a.astype(F32) + b.astype(F32)).astype(BF16)


def on_device(queries, key_states, values, grad_out, picked_blocks):
    tokens, heads, width = queries.shape
    blocks = tokens // BLK
    group = lax.axis_index("y")
    core = lax.axis_index("c").astype(jnp.int32)
    home = lax.axis_index("zl").astype(jnp.int32)
    own_keys = lax.dynamic_index_in_dim(key_states, group, 1, keepdims=False)
    own_values = lax.dynamic_index_in_dim(values, group, 1, keepdims=False)
    own = jnp.concatenate([own_keys, own_values], axis=1).reshape(1, blocks, BLK, 2 * width)
    picks = lax.dynamic_index_in_dim(picked_blocks, group, 1, keepdims=False)

    live = picks >= 0
    run = picks // blocks
    ahead = lax.rem(run // NC % ZL - home + ZL, ZL)
    holder = (ahead < NEAR).astype(jnp.int32)
    step = jnp.where(holder == 1, ahead, ZL - 1 - ahead)
    which = jnp.where(run % NC == holder, 0, 1)
    peer = run // (ZL * NC) * NC + holder
    place = jnp.where(live, peer * ZL + step * NC + which, -1)
    match = place[:, 1:, None] == jnp.arange(NX * ZL * NC, dtype=jnp.int32)
    wanted = jnp.max(jnp.where(match, (picks % blocks)[:, 1:, None], -1), axis=(0, 1))
    wanted = wanted.reshape(NX * NC, ZL)
    asked = lax.all_to_all(wanted, XC, split_axis=0, concat_axis=0, tiled=True)

    near = [jnp.concatenate([own, send(own, swap_cores)], axis=0)]
    for turn in range(NEAR):
        near.append(send(near[-1], spread if turn < NEAR - 1 else spread_last))

    got = []
    for part in range(PARTS):
        sent = pick_blocks(part, asked, core[None], near)
        arrived = lax.all_to_all(sent, XC, split_axis=0, concat_axis=0, tiled=True)
        got.append(arrived.reshape(NX * NC * PER * NC, BLK, 2 * width))
    slots = (step // PER * (NX * NC) + peer) * (PER * NC) + step % PER * NC + which
    slots = jnp.where(live, slots, -1)
    bias = jnp.where(live, 0.0, NEG).astype(F32)
    bias = jnp.broadcast_to(bias[:, :, None], (blocks, KSEL, BLK * heads))
    dq, own_grads, *back = attend_grads(
        slots, queries.reshape(tokens * heads, width), grad_out.reshape(tokens * heads, width), own[0], bias, got
    )
    grad_queries = dq.reshape(tokens, heads, width)

    sums = [None] * NEAR
    for part in reversed(range(PARTS)):
        parts = back[part].reshape(NX * NC, PER * NC, BLK, 2 * width)
        parts = lax.all_to_all(parts, XC, split_axis=0, concat_axis=0, tiled=True)
        sums[part * PER : (part + 1) * PER] = sum_parts(part, asked, parts, blocks)
    chain = sums[NEAR - 1]
    for turn in range(NEAR - 2, -1, -1):
        chain = plus(send(chain, collect), sums[turn])
    same = send(chain[0], collect_same)
    cross = send(chain[1], collect_cross)
    same = jnp.where(core == 0, same, chain[0])
    total = own_grads + same.astype(F32) + cross.astype(F32)

    pieces = total.astype(BF16).reshape(NY * ZH, tokens // (NY * ZH), 2 * width)
    pieces = lax.all_to_all(pieces, HEAD, split_axis=0, concat_axis=0, tiled=True)
    summed = pieces.astype(F32).reshape(NY, ZH, tokens // (NY * ZH), 2 * width).sum(axis=1)
    summed = summed.transpose(1, 0, 2)
    return (grad_queries, summed[:, :, :width], summed[:, :, width:])


def solution(mesh):
    torus = Mesh(mesh.devices.reshape(NX, ZL, NC, NY, ZH), AXES)
    by_head = P(SEQ, HEAD, None)
    by_run = P(SEQ, None, None)
    by_all = P(AXES, None, None)
    return jax.shard_map(
        on_device,
        mesh=torus,
        in_specs=(by_head, by_run, by_run, by_head, by_run),
        out_specs=(by_head, by_all, by_all),
        check_vma=False,
    )
```

```python
import functools

import jax
import jax.numpy as jnp
from jax import lax
from jax.experimental import pallas as pl
from jax.experimental.pallas import tpu as pltpu
from jax.sharding import Mesh
from jax.sharding import PartitionSpec as P

BLK = 64
KSEL = 16
NEG = -1e30

NX, ZL, NC, NY, ZH = 4, 8, 2, 4, 4
NZ = ZL * ZH
SEQ = ("x", "zl", "c")
HEAD = ("y", "zh")
XC = ("x", "c")
AXES = SEQ + HEAD
NEAR = ZL // 2
PARTS = 2
PER = NEAR // PARTS

F32 = jnp.float32
BF16 = jnp.bfloat16


def number(x, z, c, y):
    return (((x * ZL + z % ZL) * NC + c) * NY + y) * ZH + z % NZ // ZL


def send(array, move):
    pairs = []
    for x in range(NX):
        for z in range(NZ):
            for c in range(NC):
                for y in range(NY):
                    to = move(c)
                    if to is not None:
                        pairs.append((number(x, z, c, y), number(x, z + to[0], to[1], y)))
    return lax.ppermute(array, AXES, pairs)


def swap_cores(c):
    return (0, 1 - c)


def spread(c):
    return (1 if c == 0 else -1, c)


def spread_last(c):
    return (1, 0) if c == 0 else None


def collect(c):
    return (-1 if c == 0 else 1, c)


def collect_same(c):
    return (-1, 0) if c == 0 else None


def collect_cross(c):
    return (-1, 1) if c == 0 else (0, 0)


def attend_body(slot_ref, q_ref, g_ref, own_ref, bias_ref, *refs):
    got_refs = refs[:PARTS]
    dq_ref, down_ref = refs[PARTS : PARTS + 2]
    back_refs = refs[PARTS + 2 : 2 * PARTS + 2]
    k_ref, v_ref = refs[2 * PARTS + 2 :]
    held = got_refs[0].shape[0]
    b = pl.program_id(0)
    rows = q_ref.shape[0]
    width = q_ref.shape[1]
    heads = rows // BLK
    factor = width ** (-0.5)

    @pl.when(b == 0)
    def _():
        for back_ref in back_refs:
            back_ref[...] = jnp.zeros_like(back_ref)

    k_ref[0:BLK, :] = own_ref[0, :, :width]
    v_ref[0:BLK, :] = own_ref[0, :, width:]
    for j in range(1, KSEL):
        slot = jnp.maximum(slot_ref[b, j], 0)
        for part, got_ref in enumerate(got_refs):

            @pl.when(slot // held == part)
            def _():
                k_ref[j * BLK : (j + 1) * BLK, :] = got_ref[slot - part * held, :, :width]
                v_ref[j * BLK : (j + 1) * BLK, :] = got_ref[slot - part * held, :, width:]

    q = q_ref[...]
    g = g_ref[...]
    k = k_ref[...]
    v = v_ref[...]
    nt = (((1,), (1,)), ((), ()))
    scores = lax.dot_general(k, q, nt, preferred_element_type=F32) * factor
    key_row = lax.broadcasted_iota(jnp.int32, (BLK, rows), 0)
    token = lax.broadcasted_iota(jnp.int32, (BLK, rows), 1) // heads
    own = jnp.where(key_row <= token, scores[:BLK], NEG)
    far = scores[BLK:].reshape(KSEL - 1, BLK, rows) + bias_ref[0, 1:][:, None, :]
    scores = jnp.concatenate([own, far.reshape((KSEL - 1) * BLK, rows)], axis=0)
    weights = jnp.exp(scores - jnp.max(scores, axis=0, keepdims=True))
    attend = weights * (1.0 / jnp.sum(weights, axis=0, keepdims=True))
    grad_prob = lax.dot_general(v, g, nt, preferred_element_type=F32)
    row_dot = jnp.sum(attend * grad_prob, axis=0, keepdims=True)
    dscore = (attend * (grad_prob - row_dot)).astype(BF16)
    tn = (((0,), (0,)), ((), ()))
    nn = (((1,), (0,)), ((), ()))
    dq = lax.dot_general(k, dscore, tn, preferred_element_type=F32) * factor
    dq_ref[...] = dq.T
    dk = lax.dot_general(dscore, q, nn, preferred_element_type=F32) * factor
    dv = lax.dot_general(attend.astype(BF16), g, nn, preferred_element_type=F32)
    down_ref[0, :, :width] = dk[:BLK]
    down_ref[0, :, width:] = dv[:BLK]
    for j in range(1, KSEL):
        slot = slot_ref[b, j]

        for part, back_ref in enumerate(back_refs):

            @pl.when((slot >= part * held) & (slot < (part + 1) * held))
            def _():
                back_ref[slot - part * held, :, :width] = dk[j * BLK : (j + 1) * BLK].astype(BF16)
                back_ref[slot - part * held, :, width:] = dv[j * BLK : (j + 1) * BLK].astype(BF16)


def attend_grads(slots, q_rows, g_rows, own, bias, got):
    blocks = slots.shape[0]
    total, width = q_rows.shape
    rows = total // blocks
    row_spec = pl.BlockSpec((rows, width), lambda b, s: (b, 0))
    own_spec = pl.BlockSpec((1, BLK, 2 * width), lambda b, s: (b, 0, 0))
    whole = pl.BlockSpec(got[0].shape, lambda b, s: (0, 0, 0))
    return pl.pallas_call(
        attend_body,
        grid_spec=pltpu.PrefetchScalarGridSpec(
            num_scalar_prefetch=1,
            grid=(blocks,),
            in_specs=[row_spec, row_spec, own_spec, pl.BlockSpec((1, KSEL, rows), lambda b, s: (b, 0, 0))]
            + [whole] * PARTS,
            out_specs=[row_spec, own_spec] + [whole] * PARTS,
            scratch_shapes=[pltpu.VMEM((KSEL * BLK, width), BF16), pltpu.VMEM((KSEL * BLK, width), BF16)],
        ),
        out_shape=[
            jax.ShapeDtypeStruct((total, width), F32),
            jax.ShapeDtypeStruct((blocks, BLK, 2 * width), F32),
        ]
        + [jax.ShapeDtypeStruct(got[0].shape, BF16)] * PARTS,
        compiler_params=pltpu.CompilerParams(dimension_semantics=("arbitrary",), vmem_limit_bytes=48 * 2**20),
        name="attend_grads",
    )(slots, q_rows, g_rows, own, bias, *got)


def pick_body(part, want_ref, core_ref, *refs):
    out_ref = refs[-1]
    for core in range(NC):

        @pl.when(core_ref[0] == core)
        def _():
            for step in range(PER):
                for which in range(NC):
                    near_ref = refs[(step + 1 - core) * NC + which]
                    for peer in range(NX * NC):
                        slot = want_ref[peer, (part * PER + step) * NC + which]
                        out_ref[peer, step * NC + which] = near_ref[jnp.maximum(slot, 0)]


def pick_blocks(part, want, core, near):
    blocks, rows, width = near[0][0].shape
    shape = (NX * NC, PER * NC, rows, width)
    spec = pl.BlockSpec((blocks, rows, width), lambda i, w, h: (0, 0, 0))
    return pl.pallas_call(
        functools.partial(pick_body, part),
        grid_spec=pltpu.PrefetchScalarGridSpec(
            num_scalar_prefetch=2,
            grid=(1,),
            in_specs=[spec] * (NC * (PER + 1)),
            out_specs=pl.BlockSpec(shape, lambda i, w, h: (0, 0, 0, 0)),
        ),
        out_shape=jax.ShapeDtypeStruct(shape, BF16),
        compiler_params=pltpu.CompilerParams(vmem_limit_bytes=32 * 2**20),
        name="pick_blocks",
    )(want, core, *sum(near[part * PER : (part + 1) * PER + 1], []))


def sum_body(part, want_ref, in_ref, *refs):
    carried_refs, out_refs, sum_ref = refs[: -1 - PER * NC], refs[-1 - PER * NC : -1], refs[-1]
    for step in range(PER):
        for which in range(NC):
            sum_ref[...] = jnp.zeros_like(sum_ref)
            for peer in range(NX * NC):
                slot = jnp.maximum(want_ref[peer, (part * PER + step) * NC + which], 0)
                sum_ref[slot] += in_ref[peer, step * NC + which].astype(F32)
            total = sum_ref[...]
            if carried_refs and step == PER - 1:
                total += carried_refs[which][...].astype(F32)
            out_refs[step * NC + which][...] = total.astype(BF16)


def sum_parts(part, want, parts, blocks, carried):
    peers, runs, rows, width = parts.shape
    shape = (blocks, rows, width)
    return pl.pallas_call(
        functools.partial(sum_body, part),
        grid_spec=pltpu.PrefetchScalarGridSpec(
            num_scalar_prefetch=1,
            grid=(1,),
            in_specs=[pl.BlockSpec(parts.shape, lambda k, w: (0, 0, 0, 0))]
            + [pl.BlockSpec(shape, lambda k, w: (0, 0, 0))] * len(carried),
            out_specs=[pl.BlockSpec(shape, lambda k, w: (0, 0, 0))] * (PER * NC),
            scratch_shapes=[pltpu.VMEM((blocks, rows, width), F32)],
        ),
        out_shape=[jax.ShapeDtypeStruct(shape, BF16)] * (PER * NC),
        compiler_params=pltpu.CompilerParams(vmem_limit_bytes=32 * 2**20),
        name="sum_parts",
    )(want, parts, *carried)


def plus(a, b):
    return (a.astype(F32) + b.astype(F32)).astype(BF16)


def on_device(queries, key_states, values, grad_out, picked_blocks):
    tokens, heads, width = queries.shape
    blocks = tokens // BLK
    group = lax.axis_index("y")
    core = lax.axis_index("c").astype(jnp.int32)
    home = lax.axis_index("zl").astype(jnp.int32)
    own_keys = lax.dynamic_index_in_dim(key_states, group, 1, keepdims=False)
    own_values = lax.dynamic_index_in_dim(values, group, 1, keepdims=False)
    own = jnp.concatenate([own_keys, own_values], axis=1).reshape(blocks, BLK, 2 * width)
    picks = lax.dynamic_index_in_dim(picked_blocks, group, 1, keepdims=False)

    live = picks >= 0
    run = picks // blocks
    ahead = lax.rem(run // NC % ZL - home + ZL, ZL)
    holder = (ahead < NEAR).astype(jnp.int32)
    step = jnp.where(holder == 1, ahead, ZL - 1 - ahead)
    which = jnp.where(run % NC == holder, 0, 1)
    peer = run // (ZL * NC) * NC + holder
    place = jnp.where(live, peer * ZL + step * NC + which, -1)
    match = place[:, 1:, None] == jnp.arange(NX * ZL * NC, dtype=jnp.int32)
    wanted = jnp.max(jnp.where(match, (picks % blocks)[:, 1:, None], -1), axis=(0, 1))
    wanted = wanted.reshape(NX * NC, ZL)
    asked = lax.all_to_all(wanted, XC, split_axis=0, concat_axis=0, tiled=True)

    near = [[own, send(own, swap_cores)]]
    for turn in range(NEAR):
        near.append([send(held, spread if turn < NEAR - 1 else spread_last) for held in near[-1]])

    got = []
    for part in range(PARTS):
        sent = pick_blocks(part, asked, core[None], near)
        arrived = lax.all_to_all(sent, XC, split_axis=0, concat_axis=0, tiled=True)
        got.append(arrived.reshape(NX * NC * PER * NC, BLK, 2 * width))
    slots = (step // PER * (NX * NC) + peer) * (PER * NC) + step % PER * NC + which
    slots = jnp.where(live, slots, -1)
    bias = jnp.where(live, 0.0, NEG).astype(F32)
    bias = jnp.broadcast_to(bias[:, :, None], (blocks, KSEL, BLK * heads))
    dq, own_grads, *back = attend_grads(
        slots, queries.reshape(tokens * heads, width), grad_out.reshape(tokens * heads, width), own, bias, got
    )
    grad_queries = dq.reshape(tokens, heads, width)

    chain = []
    for part in reversed(range(PARTS)):
        parts = back[part].reshape(NX * NC, PER * NC, BLK, 2 * width)
        parts = lax.all_to_all(parts, XC, split_axis=0, concat_axis=0, tiled=True)
        sums = sum_parts(part, asked, parts, blocks, [send(held, collect) for held in chain])
        chain = sums[(PER - 1) * NC :]
        for turn in range(PER - 2, -1, -1):
            more = sums[turn * NC : (turn + 1) * NC]
            chain = [plus(send(held, collect), new) for held, new in zip(chain, more)]
    same = send(chain[0], collect_same)
    cross = send(chain[1], collect_cross)
    same = jnp.where(core == 0, same, chain[0])
    total = own_grads + same.astype(F32) + cross.astype(F32)

    pieces = total.astype(BF16).reshape(NY * ZH, tokens // (NY * ZH), 2 * width)
    pieces = lax.all_to_all(pieces, HEAD, split_axis=0, concat_axis=0, tiled=True)
    summed = pieces.astype(F32).reshape(NY, ZH, tokens // (NY * ZH), 2 * width).sum(axis=1)
    summed = summed.transpose(1, 0, 2)
    return (grad_queries, summed[:, :, :width], summed[:, :, width:])


def solution(mesh):
    torus = Mesh(mesh.devices.reshape(NX, ZL, NC, NY, ZH), AXES)
    by_head = P(SEQ, HEAD, None)
    by_run = P(SEQ, None, None)
    by_all = P(AXES, None, None)
    return jax.shard_map(
        on_device,
        mesh=torus,
        in_specs=(by_head, by_run, by_run, by_head, by_run),
        out_specs=(by_head, by_all, by_all),
        check_vma=False,
    )
```

```python
import functools

import jax
import jax.numpy as jnp
from jax import lax
from jax.experimental import pallas as pl
from jax.experimental.pallas import tpu as pltpu
from jax.sharding import Mesh
from jax.sharding import PartitionSpec as P

BLK = 64
KSEL = 16
NEG = -1e30

NX, ZL, NC, NY, ZH = 4, 8, 2, 4, 4
NZ = ZL * ZH
SEQ = ("x", "zl", "c")
HEAD = ("y", "zh")
XC = ("x", "c")
AXES = SEQ + HEAD
AWAY = [(p + 1) // 2 if p % 2 else -(p // 2) for p in range(ZL)]
PARTS = 2
PER = ZL // PARTS

F32 = jnp.float32
BF16 = jnp.bfloat16


def number(x, z, c, y):
    return (((x * ZL + z % ZL) * NC + c) * NY + y) * ZH + z % NZ // ZL


def send(array, step):
    pairs = [
        (number(x, z, c, y), number(x, z + step, c, y))
        for x in range(NX)
        for z in range(NZ)
        for c in range(NC)
        for y in range(NY)
    ]
    return lax.ppermute(array, AXES, pairs)


def attend_body(slot_ref, q_ref, g_ref, own_ref, bias_ref, *refs):
    got_refs = refs[:PARTS]
    dq_ref, down_ref = refs[PARTS : PARTS + 2]
    back_refs = refs[PARTS + 2 : 2 * PARTS + 2]
    k_ref, v_ref = refs[2 * PARTS + 2 :]
    held = got_refs[0].shape[0]
    b = pl.program_id(0)
    rows = q_ref.shape[0]
    width = q_ref.shape[1]
    heads = rows // BLK
    factor = width ** (-0.5)

    @pl.when(b == 0)
    def _():
        for back_ref in back_refs:
            back_ref[...] = jnp.zeros_like(back_ref)

    k_ref[0:BLK, :] = own_ref[0, :, :width]
    v_ref[0:BLK, :] = own_ref[0, :, width:]
    for j in range(1, KSEL):
        slot = jnp.maximum(slot_ref[b, j], 0)
        for part, got_ref in enumerate(got_refs):

            @pl.when(slot // held == part)
            def _():
                k_ref[j * BLK : (j + 1) * BLK, :] = got_ref[slot - part * held, :, :width]
                v_ref[j * BLK : (j + 1) * BLK, :] = got_ref[slot - part * held, :, width:]

    q = q_ref[...]
    g = g_ref[...]
    k = k_ref[...]
    v = v_ref[...]
    nt = (((1,), (1,)), ((), ()))
    scores = lax.dot_general(k, q, nt, preferred_element_type=F32) * factor
    key_row = lax.broadcasted_iota(jnp.int32, (BLK, rows), 0)
    token = lax.broadcasted_iota(jnp.int32, (BLK, rows), 1) // heads
    own = jnp.where(key_row <= token, scores[:BLK], NEG)
    far = scores[BLK:].reshape(KSEL - 1, BLK, rows) + bias_ref[0, 1:][:, None, :]
    scores = jnp.concatenate([own, far.reshape((KSEL - 1) * BLK, rows)], axis=0)
    weights = jnp.exp(scores - jnp.max(scores, axis=0, keepdims=True))
    attend = weights * (1.0 / jnp.sum(weights, axis=0, keepdims=True))
    grad_prob = lax.dot_general(v, g, nt, preferred_element_type=F32)
    row_dot = jnp.sum(attend * grad_prob, axis=0, keepdims=True)
    dscore = (attend * (grad_prob - row_dot)).astype(BF16)
    tn = (((0,), (0,)), ((), ()))
    nn = (((1,), (0,)), ((), ()))
    dq = lax.dot_general(k, dscore, tn, preferred_element_type=F32) * factor
    dq_ref[...] = dq.T
    dk = lax.dot_general(dscore, q, nn, preferred_element_type=F32) * factor
    dv = lax.dot_general(attend.astype(BF16), g, nn, preferred_element_type=F32)
    down_ref[0, :, :width] = dk[:BLK]
    down_ref[0, :, width:] = dv[:BLK]
    for j in range(1, KSEL):
        slot = slot_ref[b, j]

        for part, back_ref in enumerate(back_refs):

            @pl.when((slot >= part * held) & (slot < (part + 1) * held))
            def _():
                back_ref[slot - part * held, :, :width] = dk[j * BLK : (j + 1) * BLK].astype(BF16)
                back_ref[slot - part * held, :, width:] = dv[j * BLK : (j + 1) * BLK].astype(BF16)


def attend_grads(slots, q_rows, g_rows, own, bias, got):
    blocks = slots.shape[0]
    total, width = q_rows.shape
    rows = total // blocks
    row_spec = pl.BlockSpec((rows, width), lambda b, s: (b, 0))
    own_spec = pl.BlockSpec((1, BLK, 2 * width), lambda b, s: (b, 0, 0))
    whole = pl.BlockSpec(got[0].shape, lambda b, s: (0, 0, 0))
    return pl.pallas_call(
        attend_body,
        grid_spec=pltpu.PrefetchScalarGridSpec(
            num_scalar_prefetch=1,
            grid=(blocks,),
            in_specs=[row_spec, row_spec, own_spec, pl.BlockSpec((1, KSEL, rows), lambda b, s: (b, 0, 0))]
            + [whole] * PARTS,
            out_specs=[row_spec, own_spec] + [whole] * PARTS,
            scratch_shapes=[pltpu.VMEM((KSEL * BLK, width), BF16), pltpu.VMEM((KSEL * BLK, width), BF16)],
        ),
        out_shape=[
            jax.ShapeDtypeStruct((total, width), F32),
            jax.ShapeDtypeStruct((blocks, BLK, 2 * width), F32),
        ]
        + [jax.ShapeDtypeStruct(got[0].shape, BF16)] * PARTS,
        compiler_params=pltpu.CompilerParams(dimension_semantics=("arbitrary",), vmem_limit_bytes=48 * 2**20),
        name="attend_grads",
    )(slots, q_rows, g_rows, own, bias, *got)


def pick_body(part, want_ref, *refs):
    out_ref = refs[-1]
    for place, near_ref in enumerate(refs[:-1]):
        for peer in range(NX * NC):
            slot = want_ref[peer, part * PER + place]
            out_ref[peer, place] = near_ref[jnp.maximum(slot, 0)]


def pick_blocks(part, want, near):
    blocks, rows, width = near[0].shape
    shape = (NX * NC, PER, rows, width)
    return pl.pallas_call(
        functools.partial(pick_body, part),
        grid_spec=pltpu.PrefetchScalarGridSpec(
            num_scalar_prefetch=1,
            grid=(1,),
            in_specs=[pl.BlockSpec((blocks, rows, width), lambda i, w: (0, 0, 0))] * PER,
            out_specs=pl.BlockSpec(shape, lambda i, w: (0, 0, 0, 0)),
        ),
        out_shape=jax.ShapeDtypeStruct(shape, BF16),
        compiler_params=pltpu.CompilerParams(vmem_limit_bytes=32 * 2**20),
        name="pick_blocks",
    )(want, *near[part * PER : (part + 1) * PER])


def sum_body(part, want_ref, in_ref, *refs):
    home_refs, out_refs, sum_ref = refs[: -1 - PER], refs[-1 - PER : -1], refs[-1]
    for place, out_ref in enumerate(out_refs):
        sum_ref[...] = jnp.zeros_like(sum_ref)
        for peer in range(NX * NC):
            slot = jnp.maximum(want_ref[peer, part * PER + place], 0)
            sum_ref[slot] += in_ref[peer, place].astype(F32)
        total = sum_ref[...]
        if place == 0:
            for home_ref in home_refs:
                total += home_ref[...].astype(F32)
        out_ref[...] = total.astype(out_ref.dtype)


def sum_parts(part, want, parts, blocks, home):
    peers, runs, rows, width = parts.shape
    shape = (blocks, rows, width)
    return pl.pallas_call(
        functools.partial(sum_body, part),
        grid_spec=pltpu.PrefetchScalarGridSpec(
            num_scalar_prefetch=1,
            grid=(1,),
            in_specs=[pl.BlockSpec(parts.shape, lambda k, w: (0, 0, 0, 0))]
            + [pl.BlockSpec(shape, lambda k, w: (0, 0, 0))] * len(home),
            out_specs=[pl.BlockSpec(shape, lambda k, w: (0, 0, 0))] * PER,
            scratch_shapes=[pltpu.VMEM(shape, F32)],
        ),
        out_shape=[jax.ShapeDtypeStruct(shape, BF16 if place or not home else F32) for place in range(PER)],
        compiler_params=pltpu.CompilerParams(vmem_limit_bytes=32 * 2**20),
        name="sum_parts",
    )(want, parts, *home)


def on_device(queries, key_states, values, grad_out, picked_blocks):
    tokens, heads, width = queries.shape
    blocks = tokens // BLK
    group = lax.axis_index("y")
    home = lax.axis_index("zl").astype(jnp.int32)
    own_keys = lax.dynamic_index_in_dim(key_states, group, 1, keepdims=False)
    own_values = lax.dynamic_index_in_dim(values, group, 1, keepdims=False)
    own = jnp.concatenate([own_keys, own_values], axis=1).reshape(blocks, BLK, 2 * width)
    picks = lax.dynamic_index_in_dim(picked_blocks, group, 1, keepdims=False)

    live = picks >= 0
    run = picks // blocks
    ahead = lax.rem(run // NC % ZL - home + ZL, ZL)
    place = jnp.where(ahead <= ZL // 2, jnp.maximum(2 * ahead - 1, 0), 2 * (ZL - ahead))
    peer = run // (ZL * NC) * NC + run % NC
    key = jnp.where(live, peer * ZL + place, -1)
    match = key[:, 1:, None] == jnp.arange(NX * ZL * NC, dtype=jnp.int32)
    wanted = jnp.max(jnp.where(match, (picks % blocks)[:, 1:, None], -1), axis=(0, 1))
    wanted = wanted.reshape(NX * NC, ZL)
    asked = lax.all_to_all(wanted, XC, split_axis=0, concat_axis=0, tiled=True)

    near = [own] + [send(own, -away) for away in AWAY[1:]]
    got = [None] * PARTS
    for part in reversed(range(PARTS)):
        sent = pick_blocks(part, asked, near)
        arrived = lax.all_to_all(sent, XC, split_axis=0, concat_axis=0, tiled=True)
        got[part] = arrived.reshape(NX * NC * PER, BLK, 2 * width)
    slots = (place // PER * (NX * NC) + peer) * PER + place % PER
    slots = jnp.where(live, slots, -1)
    bias = jnp.where(live, 0.0, NEG).astype(F32)
    bias = jnp.broadcast_to(bias[:, :, None], (blocks, KSEL, BLK * heads))
    dq, own_grads, *back = attend_grads(
        slots, queries.reshape(tokens * heads, width), grad_out.reshape(tokens * heads, width), own, bias, got
    )
    grad_queries = dq.reshape(tokens, heads, width)

    arrived = [own_grads]
    for part in reversed(range(PARTS)):
        parts = back[part].reshape(NX * NC, PER, BLK, 2 * width)
        parts = lax.all_to_all(parts, XC, split_axis=0, concat_axis=0, tiled=True)
        sums = sum_parts(part, asked, parts, blocks, [] if part else arrived)
        if part == 0:
            arrived = [sums[0]]
        for away, held in zip(reversed(AWAY[part * PER : (part + 1) * PER]), reversed(sums)):
            if away:
                arrived.append(send(held, away))
    total = sum(held.astype(F32) for held in arrived)

    pieces = total.astype(BF16).reshape(NY * ZH, tokens // (NY * ZH), 2 * width)
    pieces = lax.all_to_all(pieces, HEAD, split_axis=0, concat_axis=0, tiled=True)
    summed = pieces.astype(F32).reshape(NY, ZH, tokens // (NY * ZH), 2 * width).sum(axis=1)
    summed = summed.transpose(1, 0, 2)
    return (grad_queries, summed[:, :, :width], summed[:, :, width:])


def solution(mesh):
    torus = Mesh(mesh.devices.reshape(NX, ZL, NC, NY, ZH), AXES)
    by_head = P(SEQ, HEAD, None)
    by_run = P(SEQ, None, None)
    by_all = P(AXES, None, None)
    return jax.shard_map(
        on_device,
        mesh=torus,
        in_specs=(by_head, by_run, by_run, by_head, by_run),
        out_specs=(by_head, by_all, by_all),
        check_vma=False,
    )
```

```python
import functools

import jax
import jax.numpy as jnp
from jax import lax
from jax.experimental import pallas as pl
from jax.experimental.pallas import tpu as pltpu
from jax.sharding import Mesh
from jax.sharding import PartitionSpec as P

BLK = 64
KSEL = 16
NEG = -1e30

NX, ZL, NC, NY, ZH = 4, 8, 2, 4, 4
NZ = ZL * ZH
SEQ = ("x", "zl", "c")
HEAD = ("y", "zh")
XC = ("x", "c")
AXES = SEQ + HEAD
AWAY = [-(p + 1) // 2 if p % 2 else p // 2 for p in range(ZL)]
PARTS = 2
PER = ZL // PARTS

F32 = jnp.float32
BF16 = jnp.bfloat16


def number(x, z, c, y):
    return (((x * ZL + z % ZL) * NC + c) * NY + y) * ZH + z % NZ // ZL


def send(array, step):
    pairs = [
        (number(x, z, c, y), number(x, z + step, c, y))
        for x in range(NX)
        for z in range(NZ)
        for c in range(NC)
        for y in range(NY)
    ]
    return lax.ppermute(array, AXES, pairs)


def attend_body(slot_ref, q_ref, g_ref, own_ref, bias_ref, *refs):
    got_refs = refs[:PARTS]
    dq_ref, down_ref = refs[PARTS : PARTS + 2]
    back_refs = refs[PARTS + 2 : 2 * PARTS + 2]
    k_ref, v_ref = refs[2 * PARTS + 2 :]
    held = got_refs[0].shape[0]
    b = pl.program_id(0)
    rows = q_ref.shape[0]
    width = q_ref.shape[1]
    heads = rows // BLK
    factor = width ** (-0.5)

    @pl.when(b == 0)
    def _():
        for back_ref in back_refs:
            back_ref[...] = jnp.zeros_like(back_ref)

    k_ref[0:BLK, :] = own_ref[0, :, :width]
    v_ref[0:BLK, :] = own_ref[0, :, width:]
    for j in range(1, KSEL):
        slot = jnp.maximum(slot_ref[b, j], 0)
        for part, got_ref in enumerate(got_refs):

            @pl.when(slot // held == part)
            def _():
                k_ref[j * BLK : (j + 1) * BLK, :] = got_ref[slot - part * held, :, :width]
                v_ref[j * BLK : (j + 1) * BLK, :] = got_ref[slot - part * held, :, width:]

    q = q_ref[...]
    g = g_ref[...]
    k = k_ref[...]
    v = v_ref[...]
    nt = (((1,), (1,)), ((), ()))
    scores = lax.dot_general(k, q, nt, preferred_element_type=F32) * factor
    key_row = lax.broadcasted_iota(jnp.int32, (BLK, rows), 0)
    token = lax.broadcasted_iota(jnp.int32, (BLK, rows), 1) // heads
    own = jnp.where(key_row <= token, scores[:BLK], NEG)
    far = scores[BLK:].reshape(KSEL - 1, BLK, rows) + bias_ref[0, 1:][:, None, :]
    scores = jnp.concatenate([own, far.reshape((KSEL - 1) * BLK, rows)], axis=0)
    weights = jnp.exp(scores - jnp.max(scores, axis=0, keepdims=True))
    attend = weights * (1.0 / jnp.sum(weights, axis=0, keepdims=True))
    grad_prob = lax.dot_general(v, g, nt, preferred_element_type=F32)
    row_dot = jnp.sum(attend * grad_prob, axis=0, keepdims=True)
    dscore = (attend * (grad_prob - row_dot)).astype(BF16)
    tn = (((0,), (0,)), ((), ()))
    nn = (((1,), (0,)), ((), ()))
    dq = lax.dot_general(k, dscore, tn, preferred_element_type=F32) * factor
    dq_ref[...] = dq.T
    dk = lax.dot_general(dscore, q, nn, preferred_element_type=F32) * factor
    dv = lax.dot_general(attend.astype(BF16), g, nn, preferred_element_type=F32)
    down_ref[0, :, :width] = dk[:BLK]
    down_ref[0, :, width:] = dv[:BLK]
    for j in range(1, KSEL):
        slot = slot_ref[b, j]

        for part, back_ref in enumerate(back_refs):

            @pl.when((slot >= part * held) & (slot < (part + 1) * held))
            def _():
                back_ref[slot - part * held, :, :width] = dk[j * BLK : (j + 1) * BLK].astype(BF16)
                back_ref[slot - part * held, :, width:] = dv[j * BLK : (j + 1) * BLK].astype(BF16)


def attend_grads(slots, q_rows, g_rows, own, bias, got):
    blocks = slots.shape[0]
    total, width = q_rows.shape
    rows = total // blocks
    row_spec = pl.BlockSpec((rows, width), lambda b, s: (b, 0))
    own_spec = pl.BlockSpec((1, BLK, 2 * width), lambda b, s: (b, 0, 0))
    whole = pl.BlockSpec(got[0].shape, lambda b, s: (0, 0, 0))
    return pl.pallas_call(
        attend_body,
        grid_spec=pltpu.PrefetchScalarGridSpec(
            num_scalar_prefetch=1,
            grid=(blocks,),
            in_specs=[row_spec, row_spec, own_spec, pl.BlockSpec((1, KSEL, rows), lambda b, s: (b, 0, 0))]
            + [whole] * PARTS,
            out_specs=[row_spec, own_spec] + [whole] * PARTS,
            scratch_shapes=[pltpu.VMEM((KSEL * BLK, width), BF16), pltpu.VMEM((KSEL * BLK, width), BF16)],
        ),
        out_shape=[
            jax.ShapeDtypeStruct((total, width), F32),
            jax.ShapeDtypeStruct((blocks, BLK, 2 * width), F32),
        ]
        + [jax.ShapeDtypeStruct(got[0].shape, BF16)] * PARTS,
        compiler_params=pltpu.CompilerParams(dimension_semantics=("arbitrary",), vmem_limit_bytes=48 * 2**20),
        name="attend_grads",
    )(slots, q_rows, g_rows, own, bias, *got)


def pick_body(part, want_ref, *refs):
    out_ref = refs[-1]
    for place, near_ref in enumerate(refs[:-1]):
        for peer in range(NX * NC):
            slot = want_ref[peer, part * PER + place]
            out_ref[peer, place] = near_ref[jnp.maximum(slot, 0)]


def pick_blocks(part, want, near):
    blocks, rows, width = near[0].shape
    shape = (NX * NC, PER, rows, width)
    return pl.pallas_call(
        functools.partial(pick_body, part),
        grid_spec=pltpu.PrefetchScalarGridSpec(
            num_scalar_prefetch=1,
            grid=(1,),
            in_specs=[pl.BlockSpec((blocks, rows, width), lambda i, w: (0, 0, 0))] * PER,
            out_specs=pl.BlockSpec(shape, lambda i, w: (0, 0, 0, 0)),
        ),
        out_shape=jax.ShapeDtypeStruct(shape, BF16),
        compiler_params=pltpu.CompilerParams(vmem_limit_bytes=32 * 2**20),
        name="pick_blocks",
    )(want, *near[part * PER : (part + 1) * PER])


def sum_body(part, want_ref, in_ref, *refs):
    carried_refs, out_refs, sum_ref = list(refs[: -1 - PER]), refs[-1 - PER : -1], refs[-1]
    carried_at = [0, PER - 2, PER - 1] if carried_refs else []
    for place, out_ref in enumerate(out_refs):
        sum_ref[...] = jnp.zeros_like(sum_ref)
        for peer in range(NX * NC):
            slot = jnp.maximum(want_ref[peer, part * PER + place], 0)
            sum_ref[slot] += in_ref[peer, place].astype(F32)
        total = sum_ref[...]
        if place in carried_at:
            total += carried_refs[carried_at.index(place)][...].astype(F32)
        out_ref[...] = total.astype(out_ref.dtype)


def sum_parts(part, want, parts, blocks, carried):
    peers, runs, rows, width = parts.shape
    shape = (blocks, rows, width)
    return pl.pallas_call(
        functools.partial(sum_body, part),
        grid_spec=pltpu.PrefetchScalarGridSpec(
            num_scalar_prefetch=1,
            grid=(1,),
            in_specs=[pl.BlockSpec(parts.shape, lambda k, w: (0, 0, 0, 0))]
            + [pl.BlockSpec(shape, lambda k, w: (0, 0, 0))] * len(carried),
            out_specs=[pl.BlockSpec(shape, lambda k, w: (0, 0, 0))] * PER,
            scratch_shapes=[pltpu.VMEM(shape, F32)],
        ),
        out_shape=[jax.ShapeDtypeStruct(shape, BF16 if place or not carried else F32) for place in range(PER)],
        compiler_params=pltpu.CompilerParams(vmem_limit_bytes=32 * 2**20),
        name="sum_parts",
    )(want, parts, *carried)


def plus(a, b):
    return (a.astype(F32) + b.astype(F32)).astype(BF16)


def on_device(queries, key_states, values, grad_out, picked_blocks):
    tokens, heads, width = queries.shape
    blocks = tokens // BLK
    group = lax.axis_index("y")
    home = lax.axis_index("zl").astype(jnp.int32)
    own_keys = lax.dynamic_index_in_dim(key_states, group, 1, keepdims=False)
    own_values = lax.dynamic_index_in_dim(values, group, 1, keepdims=False)
    own = jnp.concatenate([own_keys, own_values], axis=1).reshape(blocks, BLK, 2 * width)
    picks = lax.dynamic_index_in_dim(picked_blocks, group, 1, keepdims=False)

    live = picks >= 0
    run = picks // blocks
    ahead = lax.rem(run // NC % ZL - home + ZL, ZL)
    place = jnp.where(ahead < ZL // 2, 2 * ahead, 2 * (ZL - ahead) - 1)
    peer = run // (ZL * NC) * NC + run % NC
    key = jnp.where(live, peer * ZL + place, -1)
    match = key[:, 1:, None] == jnp.arange(NX * ZL * NC, dtype=jnp.int32)
    wanted = jnp.max(jnp.where(match, (picks % blocks)[:, 1:, None], -1), axis=(0, 1))
    wanted = wanted.reshape(NX * NC, ZL)
    asked = lax.all_to_all(wanted, XC, split_axis=0, concat_axis=0, tiled=True)

    near = [own]
    for away in AWAY[1:]:
        near.append(send(near[max(len(near) - 2, 0)], 1 if away < 0 else -1))
    got = [None] * PARTS
    for part in range(PARTS):
        sent = pick_blocks(part, asked, near)
        arrived = lax.all_to_all(sent, XC, split_axis=0, concat_axis=0, tiled=True)
        got[part] = arrived.reshape(NX * NC * PER, BLK, 2 * width)
    slots = (place // PER * (NX * NC) + peer) * PER + place % PER
    slots = jnp.where(live, slots, -1)
    bias = jnp.where(live, 0.0, NEG).astype(F32)
    bias = jnp.broadcast_to(bias[:, :, None], (blocks, KSEL, BLK * heads))
    dq, own_grads, *back = attend_grads(
        slots, queries.reshape(tokens * heads, width), grad_out.reshape(tokens * heads, width), own, bias, got
    )
    grad_queries = dq.reshape(tokens, heads, width)

    def returned(part, carried):
        parts = back[part].reshape(NX * NC, PER, BLK, 2 * width)
        parts = lax.all_to_all(parts, XC, split_axis=0, concat_axis=0, tiled=True)
        return sum_parts(part, asked, parts, blocks, carried)

    up2, down3, up3, down4 = returned(1, [])
    down = send(plus(send(down4, -1), down3), -1)
    up = send(plus(send(up3, 1), up2), 1)
    total, down1, up1, down2 = returned(0, [own_grads, up, down])
    down = send(plus(send(down2, -1), down1), -1)
    total = total + down.astype(F32) + send(up1, 1).astype(F32)

    pieces = total.astype(BF16).reshape(NY * ZH, tokens // (NY * ZH), 2 * width)
    pieces = lax.all_to_all(pieces, HEAD, split_axis=0, concat_axis=0, tiled=True)
    summed = pieces.astype(F32).reshape(NY, ZH, tokens // (NY * ZH), 2 * width).sum(axis=1)
    summed = summed.transpose(1, 0, 2)
    return (grad_queries, summed[:, :, :width], summed[:, :, width:])


def solution(mesh):
    torus = Mesh(mesh.devices.reshape(NX, ZL, NC, NY, ZH), AXES)
    by_head = P(SEQ, HEAD, None)
    by_run = P(SEQ, None, None)
    by_all = P(AXES, None, None)
    return jax.shard_map(
        on_device,
        mesh=torus,
        in_specs=(by_head, by_run, by_run, by_head, by_run),
        out_specs=(by_head, by_all, by_all),
        check_vma=False,
    )
```

```python
import jax
import jax.numpy as jnp
from jax import lax
from jax.experimental import pallas as pl
from jax.experimental.pallas import tpu as pltpu
from jax.sharding import Mesh
from jax.sharding import PartitionSpec as P

BLK = 64
KSEL = 16
NEG = -1e30

NX, ZS, ZB, NC, NY, ZH = 4, 4, 2, 2, 4, 4
NZ = ZH * ZS * ZB
SEQ = ("x", "zs", "zb", "c")
HEAD = ("y", "zh")
AXES = SEQ + HEAD
SIDE = ("x", "zb", "c")
PEERS = NX * ZB * NC
AWAY = [-(p + 1) // 2 if p % 2 else p // 2 for p in range(ZS)]

F32 = jnp.float32
BF16 = jnp.bfloat16


def number(x, z, c, y):
    run = ZS * ZB
    return (((x * run + z % run) * NC + c) * NY + y) * ZH + z % NZ // run


def send(array, step):
    pairs = [
        (number(x, z, c, y), number(x, z + step * ZB, c, y))
        for x in range(NX)
        for z in range(NZ)
        for c in range(NC)
        for y in range(NY)
    ]
    return lax.ppermute(array, AXES, pairs)


def attend_body(slot_ref, q_ref, g_ref, own_ref, bias_ref, got_ref, dq_ref, down_ref, back_ref, k_ref, v_ref):
    b = pl.program_id(0)
    rows = q_ref.shape[0]
    width = q_ref.shape[1]
    heads = rows // BLK
    factor = width ** (-0.5)

    @pl.when(b == 0)
    def _():
        back_ref[...] = jnp.zeros_like(back_ref)

    k_ref[0:BLK, :] = own_ref[0, :, :width]
    v_ref[0:BLK, :] = own_ref[0, :, width:]
    for j in range(1, KSEL):
        slot = jnp.maximum(slot_ref[b, j], 0)
        k_ref[j * BLK : (j + 1) * BLK, :] = got_ref[slot, :, :width]
        v_ref[j * BLK : (j + 1) * BLK, :] = got_ref[slot, :, width:]
    q = q_ref[...]
    g = g_ref[...]
    k = k_ref[...]
    v = v_ref[...]
    nt = (((1,), (1,)), ((), ()))
    scores = lax.dot_general(k, q, nt, preferred_element_type=F32) * factor
    key_row = lax.broadcasted_iota(jnp.int32, (BLK, rows), 0)
    token = lax.broadcasted_iota(jnp.int32, (BLK, rows), 1) // heads
    own = jnp.where(key_row <= token, scores[:BLK], NEG)
    far = scores[BLK:].reshape(KSEL - 1, BLK, rows) + bias_ref[0, 1:][:, None, :]
    scores = jnp.concatenate([own, far.reshape((KSEL - 1) * BLK, rows)], axis=0)
    weights = jnp.exp(scores - jnp.max(scores, axis=0, keepdims=True))
    attend = weights * (1.0 / jnp.sum(weights, axis=0, keepdims=True))
    grad_prob = lax.dot_general(v, g, nt, preferred_element_type=F32)
    row_dot = jnp.sum(attend * grad_prob, axis=0, keepdims=True)
    dscore = (attend * (grad_prob - row_dot)).astype(BF16)
    tn = (((0,), (0,)), ((), ()))
    nn = (((1,), (0,)), ((), ()))
    dq = lax.dot_general(k, dscore, tn, preferred_element_type=F32) * factor
    dq_ref[...] = dq.T
    dk = lax.dot_general(dscore, q, nn, preferred_element_type=F32) * factor
    dv = lax.dot_general(attend.astype(BF16), g, nn, preferred_element_type=F32)
    down_ref[0, :, :width] = dk[:BLK]
    down_ref[0, :, width:] = dv[:BLK]
    for j in range(1, KSEL):
        slot = slot_ref[b, j]

        @pl.when(slot >= 0)
        def _():
            back_ref[slot, :, :width] = dk[j * BLK : (j + 1) * BLK].astype(BF16)
            back_ref[slot, :, width:] = dv[j * BLK : (j + 1) * BLK].astype(BF16)


def attend_grads(slots, q_rows, g_rows, own, bias, got):
    blocks = slots.shape[0]
    total, width = q_rows.shape
    rows = total // blocks
    row_spec = pl.BlockSpec((rows, width), lambda b, s: (b, 0))
    own_spec = pl.BlockSpec((1, BLK, 2 * width), lambda b, s: (b, 0, 0))
    whole = pl.BlockSpec(got.shape, lambda b, s: (0, 0, 0))
    return pl.pallas_call(
        attend_body,
        grid_spec=pltpu.PrefetchScalarGridSpec(
            num_scalar_prefetch=1,
            grid=(blocks,),
            in_specs=[row_spec, row_spec, own_spec, pl.BlockSpec((1, KSEL, rows), lambda b, s: (b, 0, 0)), whole],
            out_specs=[row_spec, own_spec, whole],
            scratch_shapes=[pltpu.VMEM((KSEL * BLK, width), BF16), pltpu.VMEM((KSEL * BLK, width), BF16)],
        ),
        out_shape=[
            jax.ShapeDtypeStruct((total, width), F32),
            jax.ShapeDtypeStruct((blocks, BLK, 2 * width), F32),
            jax.ShapeDtypeStruct(got.shape, BF16),
        ],
        compiler_params=pltpu.CompilerParams(dimension_semantics=("arbitrary",), vmem_limit_bytes=48 * 2**20),
        name="attend_grads",
    )(slots, q_rows, g_rows, own, bias, got)


def pick_body(want_ref, *refs):
    out_ref = refs[-1]
    for place, near_ref in enumerate(refs[:-1]):
        for peer in range(PEERS):
            slot = want_ref[peer, place]
            out_ref[peer, place] = near_ref[jnp.maximum(slot, 0)]


def pick_blocks(want, near):
    blocks, rows, width = near[0].shape
    shape = (PEERS, ZS, rows, width)
    return pl.pallas_call(
        pick_body,
        grid_spec=pltpu.PrefetchScalarGridSpec(
            num_scalar_prefetch=1,
            grid=(1,),
            in_specs=[pl.BlockSpec((blocks, rows, width), lambda i, w: (0, 0, 0))] * ZS,
            out_specs=pl.BlockSpec(shape, lambda i, w: (0, 0, 0, 0)),
        ),
        out_shape=jax.ShapeDtypeStruct(shape, BF16),
        compiler_params=pltpu.CompilerParams(vmem_limit_bytes=32 * 2**20),
        name="pick_blocks",
    )(want, *near)


def sum_body(want_ref, in_ref, own_ref, *refs):
    out_refs, sum_ref = refs[:-1], refs[-1]
    for place, out_ref in enumerate(out_refs):
        sum_ref[...] = jnp.zeros_like(sum_ref) if place else own_ref[...]
        for peer in range(PEERS):
            slot = jnp.maximum(want_ref[peer, place], 0)
            sum_ref[slot] += in_ref[peer, place].astype(F32)
        out_ref[...] = sum_ref[...].astype(out_ref.dtype)


def sum_parts(want, parts, own_grads):
    shape = own_grads.shape
    spec = pl.BlockSpec(shape, lambda k, w: (0, 0, 0))
    return pl.pallas_call(
        sum_body,
        grid_spec=pltpu.PrefetchScalarGridSpec(
            num_scalar_prefetch=1,
            grid=(1,),
            in_specs=[pl.BlockSpec(parts.shape, lambda k, w: (0, 0, 0, 0)), spec],
            out_specs=[spec] * ZS,
            scratch_shapes=[pltpu.VMEM(shape, F32)],
        ),
        out_shape=[jax.ShapeDtypeStruct(shape, BF16 if place else F32) for place in range(ZS)],
        compiler_params=pltpu.CompilerParams(vmem_limit_bytes=32 * 2**20),
        name="sum_parts",
    )(want, parts, own_grads)


def plus(a, b):
    return (a.astype(F32) + b.astype(F32)).astype(BF16)


def on_device(queries, key_states, values, grad_out, picked_blocks):
    tokens, heads, width = queries.shape
    blocks = tokens // BLK
    group = lax.axis_index("y")
    home = lax.axis_index("zs").astype(jnp.int32)
    own_keys = lax.dynamic_index_in_dim(key_states, group, 1, keepdims=False)
    own_values = lax.dynamic_index_in_dim(values, group, 1, keepdims=False)
    own = jnp.concatenate([own_keys, own_values], axis=1).reshape(blocks, BLK, 2 * width)
    picks = lax.dynamic_index_in_dim(picked_blocks, group, 1, keepdims=False)

    live = picks >= 0
    run = picks // blocks
    ahead = lax.rem(run // (ZB * NC) % ZS - home + ZS, ZS)
    place = jnp.where(ahead < ZS // 2, 2 * ahead, 2 * (ZS - ahead) - 1)
    peer = run // (ZS * ZB * NC) * (ZB * NC) + run % (ZB * NC)
    slots = jnp.where(live, peer * ZS + place, -1)
    match = slots[:, 1:, None] == jnp.arange(PEERS * ZS, dtype=jnp.int32)
    wanted = jnp.max(jnp.where(match, (picks % blocks)[:, 1:, None], -1), axis=(0, 1))
    asked = lax.all_to_all(wanted.reshape(PEERS, ZS), SIDE, split_axis=0, concat_axis=0, tiled=True)

    near = [own]
    for away in AWAY[1:]:
        near.append(send(near[max(len(near) - 2, 0)], 1 if away < 0 else -1))
    got = lax.all_to_all(pick_blocks(asked, near), SIDE, split_axis=0, concat_axis=0, tiled=True)
    got = got.reshape(PEERS * ZS, BLK, 2 * width)
    bias = jnp.where(live, 0.0, NEG).astype(F32)
    bias = jnp.broadcast_to(bias[:, :, None], (blocks, KSEL, BLK * heads))
    dq, own_grads, back = attend_grads(
        slots, queries.reshape(tokens * heads, width), grad_out.reshape(tokens * heads, width), own, bias, got
    )
    grad_queries = dq.reshape(tokens, heads, width)

    parts = lax.all_to_all(back.reshape(PEERS, ZS, BLK, 2 * width), SIDE, split_axis=0, concat_axis=0, tiled=True)
    total, down1, up1, down2 = sum_parts(asked, parts, own_grads)
    down = send(plus(send(down2, -1), down1), -1)
    total = total + down.astype(F32) + send(up1, 1).astype(F32)

    pieces = total.astype(BF16).reshape(NY * ZH, tokens // (NY * ZH), 2 * width)
    pieces = lax.all_to_all(pieces, HEAD, split_axis=0, concat_axis=0, tiled=True)
    summed = pieces.astype(F32).reshape(NY, ZH, tokens // (NY * ZH), 2 * width).sum(axis=1)
    summed = summed.transpose(1, 0, 2)
    return (grad_queries, summed[:, :, :width], summed[:, :, width:])


def solution(mesh):
    torus = Mesh(mesh.devices.reshape(NX, ZS, ZB, NC, NY, ZH), AXES)
    by_head = P(SEQ, HEAD, None)
    by_run = P(SEQ, None, None)
    by_all = P(AXES, None, None)
    return jax.shard_map(
        on_device,
        mesh=torus,
        in_specs=(by_head, by_run, by_run, by_head, by_run),
        out_specs=(by_head, by_all, by_all),
        check_vma=False,
    )
```

```python
import functools
import math

import jax
import jax.numpy as jnp
from jax import lax
from jax.experimental import pallas as pl
from jax.experimental.pallas import tpu as pltpu
from jax.sharding import Mesh
from jax.sharding import PartitionSpec as P

BLK = 64
KSEL = 16
NEG = -1e30

NX, ZS, ZB, NC, NY, ZH = 4, 4, 2, 2, 4, 4
NZ = ZH * ZS * ZB
SEQ = ("x", "zs", "zb", "c")
HEAD = ("y", "zh")
AXES = SEQ + HEAD
SIDE = ("x", "zb", "c")
PEERS = NX * ZB * NC
PER = ZS // 2
AWAY = [-(p + 1) // 2 if p % 2 else p // 2 for p in range(ZS)]

F32 = jnp.float32
BF16 = jnp.bfloat16


def number(x, z, c, y):
    run = ZS * ZB
    return (((x * run + z % run) * NC + c) * NY + y) * ZH + z % NZ // run


def send(array, step):
    pairs = [
        (number(x, z, c, y), number(x, z + step * ZB, c, y))
        for x in range(NX)
        for z in range(NZ)
        for c in range(NC)
        for y in range(NY)
    ]
    return lax.ppermute(array, AXES, pairs)


def attend_body(slot_ref, q_ref, g_ref, own_ref, bias_ref, got_ref, dq_ref, down_ref, *refs):
    *out_refs, k_ref, v_ref, back_ref = refs
    b = pl.program_id(0)
    rows = q_ref.shape[0]
    width = q_ref.shape[1]
    heads = rows // BLK
    factor = width ** (-0.5)

    @pl.when(b == 0)
    def _():
        back_ref[...] = jnp.zeros_like(back_ref)

    k_ref[0:BLK, :] = own_ref[0, :, :width]
    v_ref[0:BLK, :] = own_ref[0, :, width:]
    for j in range(1, KSEL):
        slot = jnp.maximum(slot_ref[b, j], 0)
        k_ref[j * BLK : (j + 1) * BLK, :] = got_ref[slot, :, :width]
        v_ref[j * BLK : (j + 1) * BLK, :] = got_ref[slot, :, width:]
    q = q_ref[...]
    g = g_ref[...]
    k = k_ref[...]
    v = v_ref[...]
    nt = (((1,), (1,)), ((), ()))
    scores = lax.dot_general(k, q, nt, preferred_element_type=F32)
    key_row = lax.broadcasted_iota(jnp.int32, (BLK, rows), 0)
    token = lax.broadcasted_iota(jnp.int32, (BLK, rows), 1) // heads
    own = jnp.where(key_row <= token, scores[:BLK], NEG)
    far = scores[BLK:].reshape(KSEL - 1, BLK, rows) + bias_ref[0, 1:][:, None, :]
    scores = jnp.concatenate([own, far.reshape((KSEL - 1) * BLK, rows)], axis=0)
    weights = jnp.exp2((scores - jnp.max(scores, axis=0, keepdims=True)) * (factor * math.log2(math.e)))
    attend = weights * (1.0 / jnp.sum(weights, axis=0, keepdims=True))
    grad_prob = lax.dot_general(v, g, nt, preferred_element_type=F32)
    row_dot = jnp.sum(attend * grad_prob, axis=0, keepdims=True)
    dscore = (attend * (grad_prob - row_dot)).astype(BF16)
    tn = (((0,), (0,)), ((), ()))
    nn = (((1,), (0,)), ((), ()))
    dq = lax.dot_general(k, dscore, tn, preferred_element_type=F32) * factor
    dq_ref[...] = dq.T
    dk = lax.dot_general(dscore, q, nn, preferred_element_type=F32) * factor
    dv = lax.dot_general(attend.astype(BF16), g, nn, preferred_element_type=F32)
    down_ref[0, :, :width] = dk[:BLK]
    down_ref[0, :, width:] = dv[:BLK]
    for j in range(1, KSEL):
        slot = slot_ref[b, j]
        peer, place = slot // ZS, slot % ZS
        spare = len(out_refs) * PEERS * PER
        slot = jnp.where(slot < 0, spare, (place // PER * PEERS + peer) * PER + place % PER)
        back_ref[slot, :, :width] = dk[j * BLK : (j + 1) * BLK].astype(BF16)
        back_ref[slot, :, width:] = dv[j * BLK : (j + 1) * BLK].astype(BF16)

    @pl.when(b == pl.num_programs(0) - 1)
    def _():
        for part, out_ref in enumerate(out_refs):
            out_ref[...] = back_ref[part * PEERS * PER : (part + 1) * PEERS * PER]


def attend_grads(slots, q_rows, g_rows, own, bias, got):
    blocks = slots.shape[0]
    total, width = q_rows.shape
    rows = total // blocks
    row_spec = pl.BlockSpec((rows, width), lambda b, s: (b, 0))
    own_spec = pl.BlockSpec((1, BLK, 2 * width), lambda b, s: (b, 0, 0))
    whole = pl.BlockSpec(got.shape, lambda b, s: (0, 0, 0))
    parts = got.shape[0] // (PEERS * PER)
    back = (PEERS * PER, BLK, 2 * width)
    return pl.pallas_call(
        attend_body,
        grid_spec=pltpu.PrefetchScalarGridSpec(
            num_scalar_prefetch=1,
            grid=(blocks,),
            in_specs=[row_spec, row_spec, own_spec, pl.BlockSpec((1, KSEL, rows), lambda b, s: (b, 0, 0)), whole],
            out_specs=[row_spec, own_spec] + [pl.BlockSpec(back, lambda b, s: (0, 0, 0))] * parts,
            scratch_shapes=[
                pltpu.VMEM((KSEL * BLK, width), BF16),
                pltpu.VMEM((KSEL * BLK, width), BF16),
                pltpu.VMEM((parts * PEERS * PER + 1, BLK, 2 * width), BF16),
            ],
        ),
        out_shape=[
            jax.ShapeDtypeStruct((total, width), F32),
            jax.ShapeDtypeStruct((blocks, BLK, 2 * width), F32),
        ]
        + [jax.ShapeDtypeStruct(back, BF16)] * parts,
        compiler_params=pltpu.CompilerParams(dimension_semantics=("arbitrary",), vmem_limit_bytes=48 * 2**20),
        name="attend_grads",
    )(slots, q_rows, g_rows, own, bias, got)


def pick_body(want_ref, *refs):
    out_ref = refs[-1]
    for place, near_ref in enumerate(refs[:-1]):
        for peer in range(PEERS):
            slot = want_ref[peer, place]
            out_ref[peer, place] = near_ref[jnp.maximum(slot, 0)]


def pick_blocks(want, near):
    blocks, rows, width = near[0].shape
    shape = (PEERS, ZS, rows, width)
    return pl.pallas_call(
        pick_body,
        grid_spec=pltpu.PrefetchScalarGridSpec(
            num_scalar_prefetch=1,
            grid=(1,),
            in_specs=[pl.BlockSpec((blocks, rows, width), lambda i, w: (0, 0, 0))] * ZS,
            out_specs=pl.BlockSpec(shape, lambda i, w: (0, 0, 0, 0)),
        ),
        out_shape=jax.ShapeDtypeStruct(shape, BF16),
        compiler_params=pltpu.CompilerParams(vmem_limit_bytes=32 * 2**20),
        name="pick_blocks",
    )(want, *near)


def sum_body(part, want_ref, in_ref, *refs):
    home_refs, out_refs, sum_ref = refs[: -1 - PER], refs[-1 - PER : -1], refs[-1]
    for place, out_ref in enumerate(out_refs):
        joined = (home_refs[-1:] if place else home_refs[:-1]) if home_refs else ()
        sum_ref[...] = sum((ref[...].astype(F32) for ref in joined), jnp.zeros_like(sum_ref))
        for peer in range(PEERS):
            slot = jnp.maximum(want_ref[peer, part * PER + place], 0)
            sum_ref[slot] += in_ref[peer, place].astype(F32)
        out_ref[...] = sum_ref[...].astype(out_ref.dtype)


def sum_parts(part, want, parts, shape, home):
    spec = pl.BlockSpec(shape, lambda k, w: (0, 0, 0))
    return pl.pallas_call(
        functools.partial(sum_body, part),
        grid_spec=pltpu.PrefetchScalarGridSpec(
            num_scalar_prefetch=1,
            grid=(1,),
            in_specs=[pl.BlockSpec(parts.shape, lambda k, w: (0, 0, 0, 0))] + [spec] * len(home),
            out_specs=[spec] * PER,
            scratch_shapes=[pltpu.VMEM(shape, F32)],
        ),
        out_shape=[jax.ShapeDtypeStruct(shape, F32 if home and place == 0 else BF16) for place in range(PER)],
        compiler_params=pltpu.CompilerParams(vmem_limit_bytes=32 * 2**20),
        name="sum_parts",
    )(want, parts, *home)


def on_device(queries, key_states, values, grad_out, picked_blocks):
    tokens, heads, width = queries.shape
    blocks = tokens // BLK
    group = lax.axis_index("y")
    home = lax.axis_index("zs").astype(jnp.int32)
    own_keys = lax.dynamic_index_in_dim(key_states, group, 1, keepdims=False)
    own_values = lax.dynamic_index_in_dim(values, group, 1, keepdims=False)
    own = jnp.concatenate([own_keys, own_values], axis=1).reshape(blocks, BLK, 2 * width)
    picks = lax.dynamic_index_in_dim(picked_blocks, group, 1, keepdims=False)

    live = picks >= 0
    run = picks // blocks
    ahead = lax.rem(run // (ZB * NC) % ZS - home + ZS, ZS)
    place = jnp.where(ahead < ZS // 2, 2 * ahead, 2 * (ZS - ahead) - 1)
    peer = run // (ZS * ZB * NC) * (ZB * NC) + run % (ZB * NC)
    slots = jnp.where(live, peer * ZS + place, -1)
    match = slots[:, 1:, None] == jnp.arange(PEERS * ZS, dtype=jnp.int32)
    wanted = jnp.max(jnp.where(match, (picks % blocks)[:, 1:, None], -1), axis=(0, 1))
    asked = lax.all_to_all(wanted.reshape(PEERS, ZS), SIDE, split_axis=0, concat_axis=0, tiled=True)

    near = [own] + [send(own, -away) for away in AWAY[1:]]
    got = lax.all_to_all(pick_blocks(asked, near), SIDE, split_axis=0, concat_axis=0, tiled=True)
    got = got.reshape(PEERS * ZS, BLK, 2 * width)
    bias = jnp.where(live, 0.0, NEG).astype(F32)
    bias = jnp.broadcast_to(bias[:, :, None], (blocks, KSEL, BLK * heads))
    dq, own_grads, *back = attend_grads(
        slots, queries.reshape(tokens * heads, width), grad_out.reshape(tokens * heads, width), own, bias, got
    )
    grad_queries = dq.reshape(tokens, heads, width)

    def returned(part, home):
        parts = back[part].reshape(PEERS, PER, BLK, 2 * width)
        parts = lax.all_to_all(parts, SIDE, split_axis=0, concat_axis=0, tiled=True)
        return sum_parts(part, asked, parts, own.shape, home)

    up1, down2 = returned(1, [])
    total, down1 = returned(0, [own_grads, send(up1, 1), send(down2, -1)])
    total = total + send(down1, -1).astype(F32)

    pieces = total.astype(BF16).reshape(NY * ZH, tokens // (NY * ZH), 2 * width)
    pieces = lax.all_to_all(pieces, HEAD, split_axis=0, concat_axis=0, tiled=True)
    summed = pieces.astype(F32).reshape(NY, ZH, tokens // (NY * ZH), 2 * width).sum(axis=1)
    summed = summed.transpose(1, 0, 2)
    return (grad_queries, summed[:, :, :width], summed[:, :, width:])


def solution(mesh):
    torus = Mesh(mesh.devices.reshape(NX, ZS, ZB, NC, NY, ZH), AXES)
    by_head = P(SEQ, HEAD, None)
    by_run = P(SEQ, None, None)
    by_all = P(AXES, None, None)
    return jax.shard_map(
        on_device,
        mesh=torus,
        in_specs=(by_head, by_run, by_run, by_head, by_run),
        out_specs=(by_head, by_all, by_all),
        check_vma=False,
    )
```

```python
import math

import jax
import jax.numpy as jnp
from jax import lax
from jax.experimental import pallas as pl
from jax.experimental.pallas import tpu as pltpu
from jax.sharding import Mesh
from jax.sharding import PartitionSpec as P

BLK = 64
KSEL = 16
NEG = -1e30

NX, ZS, ZB, NC, NY, ZH = 4, 4, 2, 2, 4, 4
NZ = ZH * ZS * ZB
SEQ = ("x", "zs", "zb", "c")
HEAD = ("y", "zh")
AXES = SEQ + HEAD
SIDE = ("x", "zb", "c")
PEERS = NX * ZB * NC
AWAY = [-(p + 1) // 2 if p % 2 else p // 2 for p in range(ZS)]

F32 = jnp.float32
BF16 = jnp.bfloat16


def number(x, z, c, y):
    run = ZS * ZB
    return (((x * run + z % run) * NC + c) * NY + y) * ZH + z % NZ // run


def send(array, step):
    sign = (1, -1) if abs(step) == ZS // 2 else (1, 1)
    pairs = [
        (number(x, z, c, y), number(x, z + sign[c] * step * ZB, c, y))
        for x in range(NX)
        for z in range(NZ)
        for c in range(NC)
        for y in range(NY)
    ]
    return lax.ppermute(array, AXES, pairs)


def attend_body(slot_ref, q_ref, g_ref, own_ref, bias_ref, got_ref, dq_ref, down_ref, back_ref, k_ref, v_ref):
    b = pl.program_id(0)
    rows = q_ref.shape[0]
    width = q_ref.shape[1]
    heads = rows // BLK
    factor = width ** (-0.5)

    @pl.when(b == 0)
    def _():
        back_ref[...] = jnp.zeros_like(back_ref)

    k_ref[0:BLK, :] = own_ref[0, :, :width]
    v_ref[0:BLK, :] = own_ref[0, :, width:]
    for j in range(1, KSEL):
        slot = jnp.maximum(slot_ref[b, j], 0)
        k_ref[j * BLK : (j + 1) * BLK, :] = got_ref[slot, :, :width]
        v_ref[j * BLK : (j + 1) * BLK, :] = got_ref[slot, :, width:]
    q = q_ref[...]
    g = g_ref[...]
    k = k_ref[...]
    v = v_ref[...]
    nt = (((1,), (1,)), ((), ()))
    scores = lax.dot_general(k, q, nt, preferred_element_type=F32)
    key_row = lax.broadcasted_iota(jnp.int32, (BLK, rows), 0)
    token = lax.broadcasted_iota(jnp.int32, (BLK, rows), 1) // heads
    own = jnp.where(key_row <= token, scores[:BLK], NEG)
    far = scores[BLK:].reshape(KSEL - 1, BLK, rows) + bias_ref[0, 1:][:, None, :]
    scores = jnp.concatenate([own, far.reshape((KSEL - 1) * BLK, rows)], axis=0)
    weights = jnp.exp2((scores - jnp.max(scores, axis=0, keepdims=True)) * (factor * math.log2(math.e)))
    attend = weights * (1.0 / jnp.sum(weights, axis=0, keepdims=True))
    grad_prob = lax.dot_general(v, g, nt, preferred_element_type=F32)
    row_dot = jnp.sum(attend * grad_prob, axis=0, keepdims=True)
    dscore = (attend * (grad_prob - row_dot)).astype(BF16)
    tn = (((0,), (0,)), ((), ()))
    nn = (((1,), (0,)), ((), ()))
    dq = lax.dot_general(k, dscore, tn, preferred_element_type=F32) * factor
    dq_ref[...] = dq.T
    dk = lax.dot_general(dscore, q, nn, preferred_element_type=F32) * factor
    dv = lax.dot_general(attend.astype(BF16), g, nn, preferred_element_type=F32)
    down_ref[0, :, :width] = dk[:BLK]
    down_ref[0, :, width:] = dv[:BLK]
    for j in range(1, KSEL):
        slot = slot_ref[b, j]

        @pl.when(slot >= 0)
        def _():
            back_ref[slot, :, :width] = dk[j * BLK : (j + 1) * BLK].astype(BF16)
            back_ref[slot, :, width:] = dv[j * BLK : (j + 1) * BLK].astype(BF16)


def attend_grads(slots, q_rows, g_rows, own, bias, got):
    blocks = slots.shape[0]
    total, width = q_rows.shape
    rows = total // blocks
    row_spec = pl.BlockSpec((rows, width), lambda b, s: (b, 0))
    own_spec = pl.BlockSpec((1, BLK, 2 * width), lambda b, s: (b, 0, 0))
    whole = pl.BlockSpec(got.shape, lambda b, s: (0, 0, 0))
    return pl.pallas_call(
        attend_body,
        grid_spec=pltpu.PrefetchScalarGridSpec(
            num_scalar_prefetch=1,
            grid=(blocks,),
            in_specs=[row_spec, row_spec, own_spec, pl.BlockSpec((1, KSEL, rows), lambda b, s: (b, 0, 0)), whole],
            out_specs=[row_spec, own_spec, whole],
            scratch_shapes=[pltpu.VMEM((KSEL * BLK, width), BF16), pltpu.VMEM((KSEL * BLK, width), BF16)],
        ),
        out_shape=[
            jax.ShapeDtypeStruct((total, width), F32),
            jax.ShapeDtypeStruct((blocks, BLK, 2 * width), F32),
            jax.ShapeDtypeStruct(got.shape, BF16),
        ],
        compiler_params=pltpu.CompilerParams(dimension_semantics=("arbitrary",), vmem_limit_bytes=48 * 2**20),
        name="attend_grads",
    )(slots, q_rows, g_rows, own, bias, got)


def pick_body(want_ref, *refs):
    out_ref = refs[-1]
    for place, near_ref in enumerate(refs[:-1]):
        for peer in range(PEERS):
            slot = want_ref[peer * 8, place]
            out_ref[peer, place] = near_ref[jnp.maximum(slot, 0)]


def pick_blocks(want, near):
    blocks, rows, width = near[0].shape
    shape = (PEERS, ZS, rows, width)
    return pl.pallas_call(
        pick_body,
        grid_spec=pltpu.PrefetchScalarGridSpec(
            num_scalar_prefetch=1,
            grid=(1,),
            in_specs=[pl.BlockSpec((blocks, rows, width), lambda i, w: (0, 0, 0))] * ZS,
            out_specs=pl.BlockSpec(shape, lambda i, w: (0, 0, 0, 0)),
        ),
        out_shape=jax.ShapeDtypeStruct(shape, BF16),
        compiler_params=pltpu.CompilerParams(vmem_limit_bytes=32 * 2**20),
        name="pick_blocks",
    )(want, *near)


def sum_body(want_ref, in_ref, own_ref, *refs):
    out_refs, sum_ref = refs[:-1], refs[-1]
    for place, out_ref in enumerate(out_refs):
        sum_ref[...] = jnp.zeros_like(sum_ref) if place else own_ref[...]
        for peer in range(PEERS):
            slot = jnp.maximum(want_ref[peer * 8, place], 0)
            sum_ref[slot] += in_ref[peer, place].astype(F32)
        out_ref[...] = sum_ref[...].astype(out_ref.dtype)


def sum_parts(want, parts, own_grads):
    shape = own_grads.shape
    spec = pl.BlockSpec(shape, lambda k, w: (0, 0, 0))
    return pl.pallas_call(
        sum_body,
        grid_spec=pltpu.PrefetchScalarGridSpec(
            num_scalar_prefetch=1,
            grid=(1,),
            in_specs=[pl.BlockSpec(parts.shape, lambda k, w: (0, 0, 0, 0)), spec],
            out_specs=[spec] * ZS,
            scratch_shapes=[pltpu.VMEM(shape, F32)],
        ),
        out_shape=[jax.ShapeDtypeStruct(shape, BF16 if place else F32) for place in range(ZS)],
        compiler_params=pltpu.CompilerParams(vmem_limit_bytes=32 * 2**20),
        name="sum_parts",
    )(want, parts, own_grads)


def on_device(queries, key_states, values, grad_out, picked_blocks):
    tokens, heads, width = queries.shape
    blocks = tokens // BLK
    group = lax.axis_index("y")
    home = lax.axis_index("zs").astype(jnp.int32)
    own_keys = lax.dynamic_index_in_dim(key_states, group, 1, keepdims=False)
    own_values = lax.dynamic_index_in_dim(values, group, 1, keepdims=False)
    own = jnp.concatenate([own_keys, own_values], axis=1).reshape(blocks, BLK, 2 * width)
    picks = lax.dynamic_index_in_dim(picked_blocks, group, 1, keepdims=False)

    live = picks >= 0
    run = picks // blocks
    ahead = lax.rem(run // (ZB * NC) % ZS - home + ZS, ZS)
    place = jnp.where(ahead < ZS // 2, 2 * ahead, 2 * (ZS - ahead) - 1)
    peer = run // (ZS * ZB * NC) * (ZB * NC) + run % (ZB * NC)
    slots = jnp.where(live, peer * ZS + place, -1)
    match = slots[:, 1:, None] == jnp.arange(PEERS * ZS, dtype=jnp.int32)
    wanted = jnp.max(jnp.where(match, (picks % blocks)[:, 1:, None], -1), axis=(0, 1))
    wanted = jnp.pad(wanted.reshape(PEERS, 1, ZS), ((0, 0), (0, 7), (0, 128 - ZS)))
    asked = lax.all_to_all(wanted, SIDE, split_axis=0, concat_axis=0, tiled=True).reshape(PEERS * 8, 128)

    near = [own] + [send(own, -away) for away in AWAY[1:]]
    got = lax.all_to_all(pick_blocks(asked, near), SIDE, split_axis=0, concat_axis=0, tiled=True)
    got = got.reshape(PEERS * ZS, BLK, 2 * width)
    bias = jnp.where(live, 0.0, NEG).astype(F32)
    bias = jnp.broadcast_to(bias[:, :, None], (blocks, KSEL, BLK * heads))
    dq, own_grads, back = attend_grads(
        slots, queries.reshape(tokens * heads, width), grad_out.reshape(tokens * heads, width), own, bias, got
    )
    grad_queries = dq.reshape(tokens, heads, width)

    parts = lax.all_to_all(back.reshape(PEERS, ZS, BLK, 2 * width), SIDE, split_axis=0, concat_axis=0, tiled=True)
    total, *sums = sum_parts(asked, parts, own_grads)
    for away, held in reversed(list(zip(AWAY[1:], sums))):
        total = total + send(held, away).astype(F32)

    pieces = total.astype(BF16).reshape(NY * ZH, tokens // (NY * ZH), 2 * width)
    pieces = lax.all_to_all(pieces, HEAD, split_axis=0, concat_axis=0, tiled=True)
    summed = pieces.astype(F32).reshape(NY, ZH, tokens // (NY * ZH), 2 * width).sum(axis=1)
    summed = summed.transpose(1, 0, 2)
    return (grad_queries, summed[:, :, :width], summed[:, :, width:])


def solution(mesh):
    torus = Mesh(mesh.devices.reshape(NX, ZS, ZB, NC, NY, ZH), AXES)
    by_head = P(SEQ, HEAD, None)
    by_run = P(SEQ, None, None)
    by_all = P(AXES, None, None)
    return jax.shard_map(
        on_device,
        mesh=torus,
        in_specs=(by_head, by_run, by_run, by_head, by_run),
        out_specs=(by_head, by_all, by_all),
        check_vma=False,
    )
```

```python
import math

import jax
import jax.numpy as jnp
from jax import lax
from jax.experimental import pallas as pl
from jax.experimental.pallas import tpu as pltpu
from jax.sharding import Mesh
from jax.sharding import PartitionSpec as P

BLK = 64
KSEL = 16
NEG = -1e30

NX, ZS, ZB, NC, NY, ZH = 4, 4, 2, 2, 4, 4
NZ = ZH * ZS * ZB
SEQ = ("x", "zs", "zb", "c")
HEAD = ("y", "zh")
AXES = SEQ + HEAD
SIDE = ("x", "zb", "c")
PEERS = NX * ZB * NC
AWAY = [-(p + 1) // 2 if p % 2 else p // 2 for p in range(ZS)]

F32 = jnp.float32
BF16 = jnp.bfloat16


def number(x, z, c, y):
    run = ZS * ZB
    return (((x * run + z % run) * NC + c) * NY + y) * ZH + z % NZ // run


def send(array, step):
    pairs = [
        (number(x, z, c, y), number(x, z + step * ZB, c, y))
        for x in range(NX)
        for z in range(NZ)
        for c in range(NC)
        for y in range(NY)
    ]
    return lax.ppermute(array, AXES, pairs)


def attend_block(b, slot_ref, q, g, own_ref, bias_ref, got_ref, back_ref, k_ref, v_ref):
    rows, width = q.shape
    heads = rows // BLK
    factor = width ** (-0.5)
    k_ref[0:BLK, :] = own_ref[b, :, :width]
    v_ref[0:BLK, :] = own_ref[b, :, width:]
    for j in range(1, KSEL):
        slot = jnp.maximum(slot_ref[b, j], 0)
        k_ref[j * BLK : (j + 1) * BLK, :] = got_ref[slot, :, :width]
        v_ref[j * BLK : (j + 1) * BLK, :] = got_ref[slot, :, width:]
    k = k_ref[...]
    v = v_ref[...]
    nt = (((1,), (1,)), ((), ()))
    scores = lax.dot_general(k, q, nt, preferred_element_type=F32)
    key_row = lax.broadcasted_iota(jnp.int32, (BLK, rows), 0)
    token = lax.broadcasted_iota(jnp.int32, (BLK, rows), 1) // heads
    own = jnp.where(key_row <= token, scores[:BLK], NEG)
    far = scores[BLK:].reshape(KSEL - 1, BLK, rows) + bias_ref[b, 1:][:, None, :]
    scores = jnp.concatenate([own, far.reshape((KSEL - 1) * BLK, rows)], axis=0)
    weights = jnp.exp2((scores - jnp.max(scores, axis=0, keepdims=True)) * (factor * math.log2(math.e)))
    attend = weights * (1.0 / jnp.sum(weights, axis=0, keepdims=True))
    grad_prob = lax.dot_general(v, g, nt, preferred_element_type=F32)
    row_dot = jnp.sum(attend * grad_prob, axis=0, keepdims=True)
    dscore = (attend * (grad_prob - row_dot)).astype(BF16)
    tn = (((0,), (0,)), ((), ()))
    nn = (((1,), (0,)), ((), ()))
    dq = lax.dot_general(k, dscore, tn, preferred_element_type=F32) * factor
    dk = lax.dot_general(dscore, q, nn, preferred_element_type=F32) * factor
    dv = lax.dot_general(attend.astype(BF16), g, nn, preferred_element_type=F32)
    for j in range(1, KSEL):
        slot = slot_ref[b, j]
        slot = jnp.where(slot < 0, got_ref.shape[0], slot)
        back_ref[slot, :, :width] = dk[j * BLK : (j + 1) * BLK].astype(BF16)
        back_ref[slot, :, width:] = dv[j * BLK : (j + 1) * BLK].astype(BF16)
    return dq.T, jnp.concatenate([dk[:BLK], dv[:BLK]], axis=1)


def attend_body(slot_ref, q_ref, g_ref, own_ref, bias_ref, got_ref, dq_ref, down_ref, out_ref, k_ref, v_ref, back_ref):
    blocks = own_ref.shape[0]
    rows = q_ref.shape[0] // blocks
    back_ref[...] = jnp.zeros_like(back_ref)
    for b in range(blocks):
        here = slice(b * rows, (b + 1) * rows)
        dq_ref[here], down_ref[b] = attend_block(
            b, slot_ref, q_ref[here], g_ref[here], own_ref, bias_ref, got_ref, back_ref, k_ref.at[b], v_ref.at[b]
        )
    out_ref[...] = back_ref[: got_ref.shape[0]]


def attend_grads(slots, q_rows, g_rows, own, bias, got):
    blocks = slots.shape[0]
    total, width = q_rows.shape

    def whole(shape):
        return pl.BlockSpec(shape, lambda i, s: (0,) * len(shape))

    outs = [
        jax.ShapeDtypeStruct((total, width), F32),
        jax.ShapeDtypeStruct((blocks, BLK, 2 * width), F32),
        jax.ShapeDtypeStruct(got.shape, BF16),
    ]
    return pl.pallas_call(
        attend_body,
        grid_spec=pltpu.PrefetchScalarGridSpec(
            num_scalar_prefetch=1,
            grid=(1,),
            in_specs=[whole(array.shape) for array in (q_rows, g_rows, own, bias, got)],
            out_specs=[whole(out.shape) for out in outs],
            scratch_shapes=[
                pltpu.VMEM((blocks, KSEL * BLK, width), BF16),
                pltpu.VMEM((blocks, KSEL * BLK, width), BF16),
                pltpu.VMEM((got.shape[0] + 1, BLK, 2 * width), BF16),
            ],
        ),
        out_shape=outs,
        compiler_params=pltpu.CompilerParams(vmem_limit_bytes=28 * 2**20),
        name="attend_grads",
    )(slots, q_rows, g_rows, own, bias, got)


def pick_body(want_ref, *refs):
    out_ref = refs[-1]
    for place, near_ref in enumerate(refs[:-1]):
        for peer in range(PEERS):
            slot = want_ref[peer, place]
            out_ref[peer, place] = near_ref[jnp.maximum(slot, 0)]


def pick_blocks(want, near):
    blocks, rows, width = near[0].shape
    shape = (PEERS, ZS, rows, width)
    return pl.pallas_call(
        pick_body,
        grid_spec=pltpu.PrefetchScalarGridSpec(
            num_scalar_prefetch=1,
            grid=(1,),
            in_specs=[pl.BlockSpec((blocks, rows, width), lambda i, w: (0, 0, 0))] * ZS,
            out_specs=pl.BlockSpec(shape, lambda i, w: (0, 0, 0, 0)),
        ),
        out_shape=jax.ShapeDtypeStruct(shape, BF16),
        compiler_params=pltpu.CompilerParams(vmem_limit_bytes=32 * 2**20),
        name="pick_blocks",
    )(want, *near)


def sum_body(want_ref, in_ref, own_ref, *refs):
    out_refs, sum_ref = refs[:-1], refs[-1]
    for place, out_ref in enumerate(out_refs):
        sum_ref[...] = jnp.zeros_like(sum_ref) if place else own_ref[...]
        for peer in range(PEERS):
            slot = jnp.maximum(want_ref[peer, place], 0)
            sum_ref[slot] += in_ref[peer, place].astype(F32)
        out_ref[...] = sum_ref[...].astype(out_ref.dtype)


def sum_parts(want, parts, own_grads):
    shape = own_grads.shape
    spec = pl.BlockSpec(shape, lambda k, w: (0, 0, 0))
    return pl.pallas_call(
        sum_body,
        grid_spec=pltpu.PrefetchScalarGridSpec(
            num_scalar_prefetch=1,
            grid=(1,),
            in_specs=[pl.BlockSpec(parts.shape, lambda k, w: (0, 0, 0, 0)), spec],
            out_specs=[spec] * ZS,
            scratch_shapes=[pltpu.VMEM(shape, F32)],
        ),
        out_shape=[jax.ShapeDtypeStruct(shape, BF16 if place else F32) for place in range(ZS)],
        compiler_params=pltpu.CompilerParams(vmem_limit_bytes=32 * 2**20),
        name="sum_parts",
    )(want, parts, own_grads)


def plus(a, b):
    return (a.astype(F32) + b.astype(F32)).astype(BF16)


def on_device(queries, key_states, values, grad_out, picked_blocks):
    tokens, heads, width = queries.shape
    blocks = tokens // BLK
    group = lax.axis_index("y")
    home = lax.axis_index("zs").astype(jnp.int32)
    own_keys = lax.dynamic_index_in_dim(key_states, group, 1, keepdims=False)
    own_values = lax.dynamic_index_in_dim(values, group, 1, keepdims=False)
    own = jnp.concatenate([own_keys, own_values], axis=1).reshape(blocks, BLK, 2 * width)
    picks = lax.dynamic_index_in_dim(picked_blocks, group, 1, keepdims=False)

    live = picks >= 0
    run = picks // blocks
    ahead = lax.rem(run // (ZB * NC) % ZS - home + ZS, ZS)
    place = jnp.where(ahead < ZS // 2, 2 * ahead, 2 * (ZS - ahead) - 1)
    peer = run // (ZS * ZB * NC) * (ZB * NC) + run % (ZB * NC)
    slots = jnp.where(live, peer * ZS + place, -1)
    match = slots[:, 1:, None] == jnp.arange(PEERS * ZS, dtype=jnp.int32)
    wanted = jnp.max(jnp.where(match, (picks % blocks)[:, 1:, None], -1), axis=(0, 1))
    wanted = jnp.broadcast_to(wanted.reshape(PEERS, ZS, 1), (PEERS, ZS, 128))
    asked = lax.all_to_all(wanted, SIDE, split_axis=0, concat_axis=0, tiled=True)[:, :, 0]

    near = [own]
    for away in AWAY[1:]:
        near.append(send(near[max(len(near) - 2, 0)], 1 if away < 0 else -1))
    got = lax.all_to_all(pick_blocks(asked, near), SIDE, split_axis=0, concat_axis=0, tiled=True)
    got = got.reshape(PEERS * ZS, BLK, 2 * width)
    bias = jnp.where(live, 0.0, NEG).astype(F32)
    bias = jnp.broadcast_to(bias[:, :, None], (blocks, KSEL, BLK * heads))
    dq, own_grads, back = attend_grads(
        slots, queries.reshape(tokens * heads, width), grad_out.reshape(tokens * heads, width), own, bias, got
    )
    grad_queries = dq.reshape(tokens, heads, width)

    parts = lax.all_to_all(back.reshape(PEERS, ZS, BLK, 2 * width), SIDE, split_axis=0, concat_axis=0, tiled=True)
    total, down1, up1, down2 = sum_parts(asked, parts, own_grads)
    down = send(plus(send(down2, -1), down1), -1)
    total = total + down.astype(F32) + send(up1, 1).astype(F32)

    pieces = total.astype(BF16).reshape(NY * ZH, tokens // (NY * ZH), 2 * width)
    pieces = lax.all_to_all(pieces, HEAD, split_axis=0, concat_axis=0, tiled=True)
    summed = pieces.astype(F32).reshape(NY, ZH, tokens // (NY * ZH), 2 * width).sum(axis=1)
    summed = summed.transpose(1, 0, 2)
    return (grad_queries, summed[:, :, :width], summed[:, :, width:])


def solution(mesh):
    torus = Mesh(mesh.devices.reshape(NX, ZS, ZB, NC, NY, ZH), AXES)
    by_head = P(SEQ, HEAD, None)
    by_run = P(SEQ, None, None)
    by_all = P(AXES, None, None)
    return jax.shard_map(
        on_device,
        mesh=torus,
        in_specs=(by_head, by_run, by_run, by_head, by_run),
        out_specs=(by_head, by_all, by_all),
        check_vma=False,
    )
```

```python
import math

import jax
import jax.numpy as jnp
from jax import lax
from jax.experimental import pallas as pl
from jax.experimental.pallas import tpu as pltpu
from jax.sharding import Mesh
from jax.sharding import PartitionSpec as P

BLK = 64
KSEL = 16
NEG = -1e30

NX, ZS, ZB, NC, NY, ZH = 4, 4, 2, 2, 4, 4
NZ = ZH * ZS * ZB
SEQ = ("x", "zs", "zb", "c")
HEAD = ("y", "zh")
AXES = SEQ + HEAD
SIDE = ("x", "zb", "c")
PEERS = NX * ZB * NC
AWAY = [-(p + 1) // 2 if p % 2 else p // 2 for p in range(ZS)]

F32 = jnp.float32
BF16 = jnp.bfloat16


def number(x, z, c, y):
    run = ZS * ZB
    return (((x * run + z % run) * NC + c) * NY + y) * ZH + z % NZ // run


def send(array, step):
    pairs = [
        (number(x, z, c, y), number(x, z + step * ZB, c, y))
        for x in range(NX)
        for z in range(NZ)
        for c in range(NC)
        for y in range(NY)
    ]
    return lax.ppermute(array, AXES, pairs)


def attend_block(b, slot_ref, q, g, own_ref, bias_ref, got_ref, back_ref, k_ref, v_ref):
    rows, width = q.shape
    heads = rows // BLK
    factor = width ** (-0.5)
    k_ref[0:BLK, :] = own_ref[b, :, :width]
    v_ref[0:BLK, :] = own_ref[b, :, width:]
    for j in range(1, KSEL):
        slot = jnp.maximum(slot_ref[b, j], 0)
        k_ref[j * BLK : (j + 1) * BLK, :] = got_ref[slot, :, :width]
        v_ref[j * BLK : (j + 1) * BLK, :] = got_ref[slot, :, width:]
    k = k_ref[...]
    v = v_ref[...]
    nt = (((1,), (1,)), ((), ()))
    scores = lax.dot_general(k, q, nt, preferred_element_type=F32)
    key_row = lax.broadcasted_iota(jnp.int32, (BLK, rows), 0)
    token = lax.broadcasted_iota(jnp.int32, (BLK, rows), 1) // heads
    own = jnp.where(key_row <= token, scores[:BLK], NEG)
    far = scores[BLK:].reshape(KSEL - 1, BLK, rows) + bias_ref[b, 1:][:, None, :]
    scores = jnp.concatenate([own, far.reshape((KSEL - 1) * BLK, rows)], axis=0)
    weights = jnp.exp2((scores - jnp.max(scores, axis=0, keepdims=True)) * (factor * math.log2(math.e)))
    attend = weights * (1.0 / jnp.sum(weights, axis=0, keepdims=True))
    grad_prob = lax.dot_general(v, g, nt, preferred_element_type=F32)
    row_dot = jnp.sum(attend * grad_prob, axis=0, keepdims=True)
    dscore = (attend * (grad_prob - row_dot)).astype(BF16)
    tn = (((0,), (0,)), ((), ()))
    nn = (((1,), (0,)), ((), ()))
    dq = lax.dot_general(k, dscore, tn, preferred_element_type=F32) * factor
    dk = lax.dot_general(dscore, q, nn, preferred_element_type=F32) * factor
    dv = lax.dot_general(attend.astype(BF16), g, nn, preferred_element_type=F32)
    for j in range(1, KSEL):
        slot = slot_ref[b, j]
        slot = jnp.where(slot < 0, got_ref.shape[0], slot)
        back_ref[slot, :, :width] = dk[j * BLK : (j + 1) * BLK].astype(BF16)
        back_ref[slot, :, width:] = dv[j * BLK : (j + 1) * BLK].astype(BF16)
    return dq.T, jnp.concatenate([dk[:BLK], dv[:BLK]], axis=1)


def attend_body(slot_ref, q_ref, g_ref, own_ref, bias_ref, got_ref, dq_ref, down_ref, out_ref, k_ref, v_ref, back_ref):
    blocks = own_ref.shape[0]
    rows = q_ref.shape[0] // blocks
    back_ref[...] = jnp.zeros_like(back_ref)
    for b in range(blocks):
        here = slice(b * rows, (b + 1) * rows)
        dq_ref[here], down_ref[b] = attend_block(
            b, slot_ref, q_ref[here], g_ref[here], own_ref, bias_ref, got_ref, back_ref, k_ref.at[b], v_ref.at[b]
        )
    out_ref[...] = back_ref[: got_ref.shape[0]]


def attend_grads(slots, q_rows, g_rows, own, bias, got):
    blocks = slots.shape[0]
    total, width = q_rows.shape

    def whole(shape):
        return pl.BlockSpec(shape, lambda i, s: (0,) * len(shape))

    outs = [
        jax.ShapeDtypeStruct((total, width), F32),
        jax.ShapeDtypeStruct((blocks, BLK, 2 * width), F32),
        jax.ShapeDtypeStruct(got.shape, BF16),
    ]
    return pl.pallas_call(
        attend_body,
        grid_spec=pltpu.PrefetchScalarGridSpec(
            num_scalar_prefetch=1,
            grid=(1,),
            in_specs=[whole(array.shape) for array in (q_rows, g_rows, own, bias, got)],
            out_specs=[whole(out.shape) for out in outs],
            scratch_shapes=[
                pltpu.VMEM((blocks, KSEL * BLK, width), BF16),
                pltpu.VMEM((blocks, KSEL * BLK, width), BF16),
                pltpu.VMEM((got.shape[0] + 1, BLK, 2 * width), BF16),
            ],
        ),
        out_shape=outs,
        compiler_params=pltpu.CompilerParams(vmem_limit_bytes=28 * 2**20),
        name="attend_grads",
    )(slots, q_rows, g_rows, own, bias, got)


def pick_body(want_ref, *refs):
    out_ref = refs[-1]
    for place, near_ref in enumerate(refs[:-1]):
        for peer in range(PEERS):
            slot = want_ref[peer, place]
            out_ref[peer, place] = near_ref[jnp.maximum(slot, 0)]


def pick_blocks(want, near):
    blocks, rows, width = near[0].shape
    shape = (PEERS, ZS, rows, width)
    return pl.pallas_call(
        pick_body,
        grid_spec=pltpu.PrefetchScalarGridSpec(
            num_scalar_prefetch=1,
            grid=(1,),
            in_specs=[pl.BlockSpec((blocks, rows, width), lambda i, w: (0, 0, 0))] * ZS,
            out_specs=pl.BlockSpec(shape, lambda i, w: (0, 0, 0, 0)),
        ),
        out_shape=jax.ShapeDtypeStruct(shape, BF16),
        compiler_params=pltpu.CompilerParams(vmem_limit_bytes=32 * 2**20),
        name="pick_blocks",
    )(want, *near)


def sum_body(want_ref, in_ref, own_ref, *refs):
    out_refs, sum_ref = refs[:-1], refs[-1]
    for place, out_ref in enumerate(out_refs):
        sum_ref[...] = jnp.zeros_like(sum_ref) if place else own_ref[...]
        for peer in range(PEERS):
            slot = jnp.maximum(want_ref[peer, place], 0)
            sum_ref[slot] += in_ref[peer, place].astype(F32)
        out_ref[...] = sum_ref[...].astype(out_ref.dtype)


def sum_parts(want, parts, own_grads):
    shape = own_grads.shape
    spec = pl.BlockSpec(shape, lambda k, w: (0, 0, 0))
    return pl.pallas_call(
        sum_body,
        grid_spec=pltpu.PrefetchScalarGridSpec(
            num_scalar_prefetch=1,
            grid=(1,),
            in_specs=[pl.BlockSpec(parts.shape, lambda k, w: (0, 0, 0, 0)), spec],
            out_specs=[spec] * ZS,
            scratch_shapes=[pltpu.VMEM(shape, F32)],
        ),
        out_shape=[jax.ShapeDtypeStruct(shape, BF16 if place else F32) for place in range(ZS)],
        compiler_params=pltpu.CompilerParams(vmem_limit_bytes=32 * 2**20),
        name="sum_parts",
    )(want, parts, own_grads)


def plus(a, b):
    return (a.astype(F32) + b.astype(F32)).astype(BF16)


def on_device(queries, key_states, values, grad_out, picked_blocks):
    tokens, heads, width = queries.shape
    blocks = tokens // BLK
    group = lax.axis_index("y")
    home = lax.axis_index("zs").astype(jnp.int32)
    own_keys = lax.dynamic_index_in_dim(key_states, group, 1, keepdims=False)
    own_values = lax.dynamic_index_in_dim(values, group, 1, keepdims=False)
    own = jnp.concatenate([own_keys, own_values], axis=1).reshape(blocks, BLK, 2 * width)
    picks = lax.dynamic_index_in_dim(picked_blocks, group, 1, keepdims=False)

    live = picks >= 0
    run = picks // blocks
    ahead = lax.rem(run // (ZB * NC) % ZS - home + ZS, ZS)
    place = jnp.where(ahead < ZS // 2, 2 * ahead, 2 * (ZS - ahead) - 1)
    peer = run // (ZS * ZB * NC) * (ZB * NC) + run % (ZB * NC)
    slots = jnp.where(live, peer * ZS + place, -1)
    match = slots[:, 1:, None] == jnp.arange(PEERS * ZS, dtype=jnp.int32)
    wanted = jnp.max(jnp.where(match, (picks % blocks)[:, 1:, None], -1), axis=(0, 1))
    asked = lax.all_to_all(wanted.reshape(PEERS, ZS), SIDE, split_axis=0, concat_axis=0, tiled=True)

    near = [own]
    for away in AWAY[1:]:
        near.append(send(near[max(len(near) - 2, 0)], 1 if away < 0 else -1))
    got = lax.all_to_all(pick_blocks(asked, near), SIDE, split_axis=0, concat_axis=0, tiled=True)
    got = got.reshape(PEERS * ZS, BLK, 2 * width)
    bias = jnp.where(live, 0.0, NEG).astype(F32)
    bias = jnp.broadcast_to(bias[:, :, None], (blocks, KSEL, BLK * heads))
    dq, own_grads, back = attend_grads(
        slots, queries.reshape(tokens * heads, width), grad_out.reshape(tokens * heads, width), own, bias, got
    )
    grad_queries = dq.reshape(tokens, heads, width)

    parts = lax.all_to_all(back.reshape(PEERS, ZS, BLK, 2 * width), SIDE, split_axis=0, concat_axis=0, tiled=True)
    total, down1, up1, down2 = sum_parts(asked, parts, own_grads)
    down = send(plus(send(down2, -1), down1), -1)
    total = total + down.astype(F32) + send(up1, 1).astype(F32)

    pieces = total.astype(BF16).reshape(NY * ZH, tokens // (NY * ZH), 2 * width)
    pieces = lax.all_to_all(pieces, HEAD, split_axis=0, concat_axis=0, tiled=True)
    summed = pieces.astype(F32).reshape(NY, ZH, tokens // (NY * ZH), 2 * width).sum(axis=1)
    summed = summed.transpose(1, 0, 2)
    return (grad_queries, summed[:, :, :width], summed[:, :, width:])


def solution(mesh):
    torus = Mesh(mesh.devices.reshape(NX, ZS, ZB, NC, NY, ZH), AXES)
    by_head = P(SEQ, HEAD, None)
    by_run = P(SEQ, None, None)
    by_all = P(AXES, None, None)
    return jax.shard_map(
        on_device,
        mesh=torus,
        in_specs=(by_head, by_run, by_run, by_head, by_run),
        out_specs=(by_head, by_all, by_all),
        check_vma=False,
    )
```

```python
import math

import jax
import jax.numpy as jnp
from jax import lax
from jax.experimental import pallas as pl
from jax.experimental.pallas import tpu as pltpu
from jax.sharding import Mesh
from jax.sharding import PartitionSpec as P

BLK = 64
KSEL = 16
NEG = -1e30

NX, ZS, ZB, NC, NY, ZH = 4, 4, 2, 2, 4, 4
NZ = ZH * ZS * ZB
SEQ = ("x", "zs", "zb", "c")
HEAD = ("y", "zh")
AXES = SEQ + HEAD
SIDE = ("x", "zb", "c")
PEERS = NX * ZB * NC
AWAY = [-(p + 1) // 2 if p % 2 else p // 2 for p in range(ZS)]

F32 = jnp.float32
BF16 = jnp.bfloat16


def number(x, z, c, y):
    run = ZS * ZB
    return (((x * run + z % run) * NC + c) * NY + y) * ZH + z % NZ // run


def send(array, step):
    pairs = [
        (number(x, z, c, y), number(x, z + step * ZB, c, y))
        for x in range(NX)
        for z in range(NZ)
        for c in range(NC)
        for y in range(NY)
    ]
    return lax.ppermute(array, AXES, pairs)


def attend_block(b, slot_ref, q, g, own_ref, bias_ref, got_ref, back_ref, k_ref, v_ref):
    rows, width = q.shape
    heads = rows // BLK
    factor = width ** (-0.5)
    k_ref[0:BLK, :] = own_ref[b, :, :width]
    v_ref[0:BLK, :] = own_ref[b, :, width:]
    for j in range(1, KSEL):
        slot = jnp.maximum(slot_ref[b, j], 0)
        k_ref[j * BLK : (j + 1) * BLK, :] = got_ref[slot, :, :width]
        v_ref[j * BLK : (j + 1) * BLK, :] = got_ref[slot, :, width:]
    k = k_ref[...]
    v = v_ref[...]
    nt = (((1,), (1,)), ((), ()))
    scores = lax.dot_general(k, q, nt, preferred_element_type=F32)
    key_row = lax.broadcasted_iota(jnp.int32, (BLK, rows), 0)
    token = lax.broadcasted_iota(jnp.int32, (BLK, rows), 1) // heads
    own = jnp.where(key_row <= token, scores[:BLK], NEG)
    far = scores[BLK:].reshape(KSEL - 1, BLK, rows) + bias_ref[b, 1:][:, None, :]
    scores = jnp.concatenate([own, far.reshape((KSEL - 1) * BLK, rows)], axis=0)
    weights = jnp.exp2((scores - jnp.max(scores, axis=0, keepdims=True)) * (factor * math.log2(math.e)))
    attend = weights * (1.0 / jnp.sum(weights, axis=0, keepdims=True))
    grad_prob = lax.dot_general(v, g, nt, preferred_element_type=F32)
    row_dot = jnp.sum(attend * grad_prob, axis=0, keepdims=True)
    dscore = (attend * (grad_prob - row_dot)).astype(BF16)
    tn = (((0,), (0,)), ((), ()))
    nn = (((1,), (0,)), ((), ()))
    dq = lax.dot_general(k, dscore, tn, preferred_element_type=F32) * factor
    dk = lax.dot_general(dscore, q, nn, preferred_element_type=F32) * factor
    dv = lax.dot_general(attend.astype(BF16), g, nn, preferred_element_type=F32)
    for j in range(1, KSEL):
        slot = slot_ref[b, j]
        slot = jnp.where(slot < 0, got_ref.shape[0], slot)
        back_ref[slot, :, :width] = dk[j * BLK : (j + 1) * BLK].astype(BF16)
        back_ref[slot, :, width:] = dv[j * BLK : (j + 1) * BLK].astype(BF16)
    return dq.T, jnp.concatenate([dk[:BLK], dv[:BLK]], axis=1)


def attend_body(slot_ref, q_ref, g_ref, own_ref, bias_ref, got_ref, dq_ref, down_ref, out_ref, k_ref, v_ref, back_ref):
    blocks = own_ref.shape[0]
    rows = q_ref.shape[0] // blocks
    back_ref[...] = jnp.zeros_like(back_ref)
    for b in range(blocks):
        here = slice(b * rows, (b + 1) * rows)
        dq_ref[here], down_ref[b] = attend_block(
            b, slot_ref, q_ref[here], g_ref[here], own_ref, bias_ref, got_ref, back_ref, k_ref.at[b], v_ref.at[b]
        )
    out_ref[...] = back_ref[: got_ref.shape[0]]


def attend_grads(slots, q_rows, g_rows, own, bias, got):
    blocks = slots.shape[0]
    total, width = q_rows.shape

    def whole(shape):
        return pl.BlockSpec(shape, lambda i, s: (0,) * len(shape))

    outs = [
        jax.ShapeDtypeStruct((total, width), F32),
        jax.ShapeDtypeStruct((blocks, BLK, 2 * width), F32),
        jax.ShapeDtypeStruct(got.shape, BF16),
    ]
    return pl.pallas_call(
        attend_body,
        grid_spec=pltpu.PrefetchScalarGridSpec(
            num_scalar_prefetch=1,
            grid=(1,),
            in_specs=[whole(array.shape) for array in (q_rows, g_rows, own, bias, got)],
            out_specs=[whole(out.shape) for out in outs],
            scratch_shapes=[
                pltpu.VMEM((blocks, KSEL * BLK, width), BF16),
                pltpu.VMEM((blocks, KSEL * BLK, width), BF16),
                pltpu.VMEM((got.shape[0] + 1, BLK, 2 * width), BF16),
            ],
        ),
        out_shape=outs,
        compiler_params=pltpu.CompilerParams(vmem_limit_bytes=28 * 2**20),
        name="attend_grads",
    )(slots, q_rows, g_rows, own, bias, got)


def pick_body(want_ref, *refs):
    out_ref = refs[-1]
    for place, near_ref in enumerate(refs[:-1]):
        for peer in range(PEERS):
            slot = want_ref[peer, place]
            out_ref[peer, place] = near_ref[jnp.maximum(slot, 0)]


def pick_blocks(want, near):
    blocks, rows, width = near[0].shape
    shape = (PEERS, ZS, rows, width)
    return pl.pallas_call(
        pick_body,
        grid_spec=pltpu.PrefetchScalarGridSpec(
            num_scalar_prefetch=1,
            grid=(1,),
            in_specs=[pl.BlockSpec((blocks, rows, width), lambda i, w: (0, 0, 0))] * ZS,
            out_specs=pl.BlockSpec(shape, lambda i, w: (0, 0, 0, 0)),
        ),
        out_shape=jax.ShapeDtypeStruct(shape, BF16),
        compiler_params=pltpu.CompilerParams(vmem_limit_bytes=32 * 2**20),
        name="pick_blocks",
    )(want, *near)


def sum_body(want_ref, in_ref, own_ref, *refs):
    out_refs, sum_ref = refs[:-1], refs[-1]
    for place, out_ref in enumerate(out_refs):
        sum_ref[...] = jnp.zeros_like(sum_ref) if place else own_ref[...]
        for peer in range(PEERS):
            slot = jnp.maximum(want_ref[peer, place], 0)
            sum_ref[slot] += in_ref[peer, place].astype(F32)
        out_ref[...] = sum_ref[...].astype(out_ref.dtype)


def sum_parts(want, parts, own_grads):
    shape = own_grads.shape
    spec = pl.BlockSpec(shape, lambda k, w: (0, 0, 0))
    return pl.pallas_call(
        sum_body,
        grid_spec=pltpu.PrefetchScalarGridSpec(
            num_scalar_prefetch=1,
            grid=(1,),
            in_specs=[pl.BlockSpec(parts.shape, lambda k, w: (0, 0, 0, 0)), spec],
            out_specs=[spec] * ZS,
            scratch_shapes=[pltpu.VMEM(shape, F32)],
        ),
        out_shape=[jax.ShapeDtypeStruct(shape, BF16 if place else F32) for place in range(ZS)],
        compiler_params=pltpu.CompilerParams(vmem_limit_bytes=32 * 2**20),
        name="sum_parts",
    )(want, parts, own_grads)


def plus(a, b):
    return (a.astype(F32) + b.astype(F32)).astype(BF16)


def heads_body(in_ref, key_ref, value_ref):
    width = key_ref.shape[2]
    for y in range(NY):
        total = in_ref[y * ZH].astype(F32)
        for zh in range(1, ZH):
            total += in_ref[y * ZH + zh].astype(F32)
        key_ref[:, y, :] = total[:, :width]
        value_ref[:, y, :] = total[:, width:]


def sum_heads(pieces, width):
    out = jax.ShapeDtypeStruct((pieces.shape[1], NY, width), F32)
    return pl.pallas_call(heads_body, out_shape=[out, out], name="sum_heads")(pieces)


def on_device(queries, key_states, values, grad_out, picked_blocks):
    tokens, heads, width = queries.shape
    blocks = tokens // BLK
    group = lax.axis_index("y")
    home = lax.axis_index("zs").astype(jnp.int32)
    own_keys = lax.dynamic_index_in_dim(key_states, group, 1, keepdims=False)
    own_values = lax.dynamic_index_in_dim(values, group, 1, keepdims=False)
    own = jnp.concatenate([own_keys, own_values], axis=1).reshape(blocks, BLK, 2 * width)
    picks = lax.dynamic_index_in_dim(picked_blocks, group, 1, keepdims=False)

    live = picks >= 0
    run = picks // blocks
    ahead = lax.rem(run // (ZB * NC) % ZS - home + ZS, ZS)
    place = jnp.where(ahead < ZS // 2, 2 * ahead, 2 * (ZS - ahead) - 1)
    peer = run // (ZS * ZB * NC) * (ZB * NC) + run % (ZB * NC)
    slots = jnp.where(live, peer * ZS + place, -1)
    match = slots[:, 1:, None] == jnp.arange(PEERS * ZS, dtype=jnp.int32)
    wanted = jnp.max(jnp.where(match, (picks % blocks)[:, 1:, None], -1), axis=(0, 1))
    asked = lax.all_to_all(wanted.reshape(PEERS, ZS), SIDE, split_axis=0, concat_axis=0, tiled=True)

    near = [own]
    for away in AWAY[1:]:
        near.append(send(near[max(len(near) - 2, 0)], 1 if away < 0 else -1))
    got = lax.all_to_all(pick_blocks(asked, near), SIDE, split_axis=0, concat_axis=0, tiled=True)
    got = got.reshape(PEERS * ZS, BLK, 2 * width)
    bias = jnp.where(live, 0.0, NEG).astype(F32)
    bias = jnp.broadcast_to(bias[:, :, None], (blocks, KSEL, BLK * heads))
    dq, own_grads, back = attend_grads(
        slots, queries.reshape(tokens * heads, width), grad_out.reshape(tokens * heads, width), own, bias, got
    )
    grad_queries = dq.reshape(tokens, heads, width)

    parts = lax.all_to_all(back.reshape(PEERS, ZS, BLK, 2 * width), SIDE, split_axis=0, concat_axis=0, tiled=True)
    total, down1, up1, down2 = sum_parts(asked, parts, own_grads)
    down = send(plus(send(down2, -1), down1), -1)
    total = total + down.astype(F32) + send(up1, 1).astype(F32)

    pieces = total.astype(BF16).reshape(NY * ZH, tokens // (NY * ZH), 2 * width)
    pieces = lax.all_to_all(pieces, HEAD, split_axis=0, concat_axis=0, tiled=True)
    return (grad_queries, *sum_heads(pieces, width))


def solution(mesh):
    torus = Mesh(mesh.devices.reshape(NX, ZS, ZB, NC, NY, ZH), AXES)
    by_head = P(SEQ, HEAD, None)
    by_run = P(SEQ, None, None)
    by_all = P(AXES, None, None)
    return jax.shard_map(
        on_device,
        mesh=torus,
        in_specs=(by_head, by_run, by_run, by_head, by_run),
        out_specs=(by_head, by_all, by_all),
        check_vma=False,
    )
```
